256 devices in a mesh: seq: 128 (over z, y_hi, x, core), head: 2 (over y_lo).
Axes of the slice: x: 4, y: 4 (y_hi: 2, y_lo: 2; y = y_hi * 2 + y_lo), z: 8, core: 2. Of those that a mesh axis runs over, the one named last changes fastest.
Arguments:
- queries: bfloat16 [16384, 2048], P(('seq', 'head')), may hold values from -8 to 8
- key_rows: bfloat16 [16384, 2048], P(('seq', 'head')), may hold values from -8 to 8
- values: bfloat16 [16384, 2048], P(('seq', 'head')), may hold values from -6 to 6
- out_grad: bfloat16 [16384, 2048], P(('seq', 'head')), may hold values from -6 to 6
Outputs:
- attended: bfloat16 [16384, 2048], P(('seq', 'head'))
- query_grad: bfloat16 [16384, 2048], P(('seq', 'head'))
- key_grad: bfloat16 [16384, 2048], P(('seq', 'head'))
- value_grad: bfloat16 [16384, 2048], P(('seq', 'head'))
The draws below stay inside these ranges and needn't reach their ends.
All inputs are finite; a program needn't handle non-finite values.
Results may differ from the reference program's by a relative error of at most 0.028.
Values may be sent and summed in bfloat16 or wider, within the bound.
A program may use at most 64 MiB of HBM per device.

```python
import math
import jax
import jax.numpy as jnp
from jax import lax

HEADS = 16
HEAD_DIM = 128
D = 2048
TOK_DEV = 128
TOKENS = 16384
LEVELS = 7


def drawn_pair(key):
    base_key = jax.random.fold_in(key, 7)
    query_key, keyrow_key = jax.random.split(base_key, 2)
    full_shape = (TOKENS, D)
    query_part = 1.6 * jnp.clip(jax.random.normal(query_key, full_shape, jnp.float32), -5.0, 5.0)
    keyrow_part = 1.6 * jnp.clip(jax.random.normal(keyrow_key, full_shape, jnp.float32), -5.0, 5.0)
    return (query_part, keyrow_part)


def draw_queries(key, part):
    return drawn_pair(key)[0].astype(jnp.bfloat16)


def draw_key_rows(key, part):
    return drawn_pair(key)[1].astype(jnp.bfloat16)


def levels(own_key, dims, pieces, low, high):
    loudness = 1.0
    for position, parts in pieces:
        draws = jax.random.uniform(jax.random.fold_in(jax.random.fold_in(own_key, 6), position), (parts,), jnp.float32, low / len(pieces), high / len(pieces))
        loudness = loudness * jnp.repeat(jnp.exp(draws), dims[position] // parts).reshape((-1,) + (1,) * (len(dims) - 1 - position))
    return loudness


def noise(stream_key, extent, deviation, bound, pieces=(), kind=jnp.bfloat16):
    level = levels(stream_key, extent, pieces, -0.22, 0.18) if pieces else 1.0
    values = jax.random.normal(stream_key, extent, jnp.float32) * deviation * level
    return jnp.minimum(jnp.maximum(values, -bound), bound).astype(kind)


def setup_inputs(seed: int = 0) -> dict:
    splits = jax.random.split(jax.random.key(seed), 5)
    queries = draw_queries(jax.random.fold_in(splits[4], 71), 0)
    key_rows = draw_key_rows(jax.random.fold_in(splits[4], 71), 0)
    values = noise(splits[2], (TOKENS, D), 1.0, 6.0, ((0, 256),))
    out_grad = noise(splits[3], (TOKENS, D), 1.0, 6.0, ((0, 256),))
    return dict(queries=queries, key_rows=key_rows, values=values, out_grad=out_grad)


ROOT_HALF = 0.7071067811865476

def rounded(blocks):
    return lax.optimization_barrier(blocks.astype(jnp.bfloat16)).astype(jnp.float32)

def pool_rows(blocks):
    widened = blocks.astype(jnp.float32)
    paired = widened.reshape((widened.shape[0] // 2, 2) + widened.shape[1:])
    return ((paired[:, 0] + paired[:, 1]) * ROOT_HALF).astype(jnp.bfloat16)

def unpool_rows(blocks):
    return jnp.repeat(blocks, 2, axis=0) * ROOT_HALF

def swap_halves(blocks, half_rows):
    grouped = blocks.reshape(blocks.shape[0] // (2 * half_rows), 2, half_rows, blocks.shape[-1])
    return grouped[:, ::-1].reshape(blocks.shape)

def head_pass(operands):
    query_head, key_head, value_head, grad_head = operands
    scale_factor = 1.0 / math.sqrt(HEAD_DIM)
    shard_rows = TOK_DEV
    half_rows = TOK_DEV // 2
    shards = TOKENS // shard_rows
    query_pool = [query_head]
    key_pool = [key_head]
    value_pool = [value_head]
    for level_no in range(1, LEVELS + 1):
        query_pool.append(pool_rows(query_pool[-1]))
        key_pool.append(pool_rows(key_pool[-1]))
        value_pool.append(pool_rows(value_pool[-1]))
    query_blk = query_head.reshape(shards, shard_rows, HEAD_DIM).astype(jnp.float32)
    key_blk = key_head.reshape(shards, shard_rows, HEAD_DIM).astype(jnp.float32)
    value_blk = value_head.reshape(shards, shard_rows, HEAD_DIM).astype(jnp.float32)
    grad_blk = grad_head.reshape(shards, shard_rows, HEAD_DIM).astype(jnp.float32)
    local_scores = jnp.einsum('nte,nue->ntu', query_blk, key_blk) * scale_factor
    row_top = lax.optimization_barrier(jnp.max(local_scores, axis=-1)).reshape(TOKENS)
    level_data = []
    for level_no in range(1, LEVELS + 1):
        group_rows = 2 ** level_no
        coarse_rows = TOKENS // group_rows
        block_count = coarse_rows // half_rows
        coarse_query = query_pool[level_no].reshape(block_count, half_rows, HEAD_DIM).astype(jnp.float32)
        sibling_keys = swap_halves(key_pool[level_no], half_rows).reshape(block_count, half_rows, HEAD_DIM).astype(jnp.float32)
        sibling_values = swap_halves(value_pool[level_no], half_rows).reshape(block_count, half_rows, HEAD_DIM).astype(jnp.float32)
        coarse_scores = jnp.einsum('ngd,ncd->ngc', coarse_query, sibling_keys) * scale_factor
        coarse_top = lax.optimization_barrier(jnp.max(coarse_scores, axis=-1))
        coarse_expo = jnp.exp(coarse_scores - coarse_top[..., None])
        coarse_total = lax.optimization_barrier(jnp.sum(coarse_expo, axis=-1)).reshape(coarse_rows)
        expo_round = rounded(coarse_expo)
        coarse_numer = jnp.einsum('ngc,ncd->ngd', expo_round, sibling_values).reshape(coarse_rows, HEAD_DIM)
        spread_top = jnp.repeat(coarse_top.reshape(coarse_rows), group_rows)
        row_top = jnp.maximum(row_top, spread_top)
        level_data.append((coarse_query, sibling_keys, sibling_values, coarse_expo, expo_round, spread_top, coarse_total, coarse_numer))
    top_blk = row_top.reshape(shards, shard_rows)
    local_expo = jnp.exp(local_scores - top_blk[..., None])
    row_total = lax.optimization_barrier(jnp.sum(local_expo, axis=-1)).reshape(TOKENS)
    numer_all = jnp.einsum('ntu,nud->ntd', rounded(local_expo), value_blk).reshape(TOKENS, HEAD_DIM)
    factors = []
    for level_no in range(1, LEVELS + 1):
        group_rows = 2 ** level_no
        record = level_data[level_no - 1]
        factor = jnp.exp(record[5] - row_top)
        row_total = row_total + factor * jnp.repeat(record[6], group_rows)
        numer_all = numer_all + factor[:, None] * jnp.repeat(record[7], group_rows, axis=0)
        factors.append(factor)
    outcome = numer_all / row_total[:, None]
    attended = outcome.astype(jnp.bfloat16)
    grad_wide = grad_head.astype(jnp.float32)
    row_dots = lax.optimization_barrier(jnp.sum(grad_wide * outcome, axis=-1))
    total_blk = row_total.reshape(shards, shard_rows)
    dots_blk = row_dots.reshape(shards, shard_rows)
    local_probs = local_expo / total_blk[..., None]
    local_dprob = jnp.einsum('ntd,nud->ntu', grad_blk, value_blk)
    dlocal = rounded(local_probs * (local_dprob - dots_blk[..., None]))
    query_acc = (jnp.einsum('ntu,nud->ntd', dlocal, key_blk) * scale_factor).reshape(TOKENS, HEAD_DIM)
    key_acc = (jnp.einsum('ntu,ntd->nud', dlocal, query_blk) * scale_factor).reshape(TOKENS, HEAD_DIM)
    value_acc = jnp.einsum('ntu,ntd->nud', rounded(local_probs), grad_blk).reshape(TOKENS, HEAD_DIM)
    level_grads = []
    for level_no in range(1, LEVELS + 1):
        group_rows = 2 ** level_no
        coarse_rows = TOKENS // group_rows
        block_count = coarse_rows // half_rows
        coarse_query, sibling_keys, sibling_values, coarse_expo, expo_round = level_data[level_no - 1][:5]
        weight = factors[level_no - 1] / row_total
        adjoint = (weight[:, None] * grad_wide).reshape(coarse_rows, group_rows, HEAD_DIM).sum(axis=1)
        adjoint_round = rounded(adjoint).reshape(block_count, half_rows, HEAD_DIM)
        offset = (weight * row_dots).reshape(coarse_rows, group_rows).sum(axis=1).reshape(block_count, half_rows)
        inner_dot = jnp.einsum('ngd,ncd->ngc', adjoint_round, sibling_values) - offset[..., None]
        dcoarse = rounded(coarse_expo * inner_dot)
        dquery_level = (jnp.einsum('ngc,ncd->ngd', dcoarse, sibling_keys) * scale_factor).reshape(coarse_rows, HEAD_DIM)
        dkey_sib = (jnp.einsum('ngc,ngd->ncd', dcoarse, coarse_query) * scale_factor).reshape(coarse_rows, HEAD_DIM)
        dvalue_sib = jnp.einsum('ngc,ngd->ncd', expo_round, adjoint_round).reshape(coarse_rows, HEAD_DIM)
        level_grads.append((dquery_level, swap_halves(dkey_sib, half_rows), swap_halves(dvalue_sib, half_rows)))
    carried_rows = TOKENS // 2 ** LEVELS
    query_carry = jnp.zeros((carried_rows, HEAD_DIM), jnp.float32)
    key_carry = jnp.zeros((carried_rows, HEAD_DIM), jnp.float32)
    value_carry = jnp.zeros((carried_rows, HEAD_DIM), jnp.float32)
    for level_no in range(LEVELS, 0, -1):
        query_carry = unpool_rows(query_carry + level_grads[level_no - 1][0])
        key_carry = unpool_rows(key_carry + level_grads[level_no - 1][1])
        value_carry = unpool_rows(value_carry + level_grads[level_no - 1][2])
    query_final = (query_acc + query_carry).astype(jnp.bfloat16)
    key_final = (key_acc + key_carry).astype(jnp.bfloat16)
    value_final = (value_acc + value_carry).astype(jnp.bfloat16)
    return (attended, query_final, key_final, value_final)

def split_heads(matrix):
    return matrix.reshape(TOKENS, HEADS, HEAD_DIM).transpose(1, 0, 2)

def join_heads(stacked):
    return stacked.transpose(1, 0, 2).reshape(TOKENS, D)

def reference(queries, key_rows, values, out_grad):
    results = lax.map(head_pass, (split_heads(queries), split_heads(key_rows), split_heads(values), split_heads(out_grad)))
    return (join_heads(results[0]), join_heads(results[1]), join_heads(results[2]), join_heads(results[3]))
```

```python
import functools
import math

import jax
import jax.numpy as jnp
import numpy as np
from jax import lax
from jax.experimental import pallas as pl
from jax.experimental.pallas import tpu as pltpu
from jax.sharding import PartitionSpec as P

MESH = pl.DeviceIdType.MESH
BF16 = jnp.bfloat16
F32 = jnp.float32
DH = 128
SCALE = 1.0 / math.sqrt(DH)
ROOT_HALF = 0.7071067811865476
LOW = -1e30
FLOOR = -1e29

PARTNERS = [(1, 0, 0, 64)]
PARTNERS += [(n, 64, 64 + 32 * (n - 2), 32) for n in (2, 3)]
PARTNERS += [(n, 96, 128 + 16 * (n - 4), 16) for n in (4, 5, 6, 7)]


def tables():
    level_of = np.zeros(128, np.int64)
    pool = np.zeros((128, 128), np.float32)
    row = 0
    for level in range(1, 8):
        for i in range(128 >> level):
            pool[row, i << level : (i + 1) << level] = 1.0
            level_of[row] = level
            row += 1
    level_of[127] = 99
    stage = np.zeros((128, 256), np.float32)
    stage_scale = np.ones(128, np.float32)
    for level, start, count in ((5, 0, 64), (6, 64, 32), (7, 96, 16)):
        per_chip = count // 8
        for r in range(count):
            chip, i = r // per_chip, r % per_chip
            if chip == 0:
                base, have = 192, 4
            elif chip == 1:
                base, have = 0, 2
            elif chip < 4:
                base, have = 64 + 32 * (chip - 2), 3
            else:
                base, have = 128 + 16 * (chip - 4), 4
            span = 1 << (level - have)
            stage[start + r, base + i * span : base + (i + 1) * span] = 1.0
            stage_scale[start + r] = 2.0 ** (-(level - have) / 2)
    fold = np.zeros((64, 256), np.float32)
    for r in range(64):
        fold[r, r] = 1.0
        for j in range(2):
            fold[r, 64 + 32 * j + r // 2] = 2.0**-0.5
        for j in range(4):
            fold[r, 128 + 16 * j + r // 4] = 0.5
    spread = np.zeros((192, 256), np.float32)
    for r in range(64):
        spread[r, 8 + r // 8] = 2.0**-1.5
    for r in range(64):
        spread[64 + r, 16 + r // 4] = 0.5
        spread[128 + r, 32 + r // 2] = 2.0**-0.5
    unfold = np.zeros((128, 256), np.float32)
    for r in range(128):
        unfold[r, r // 2] = 2.0**-0.5
        for j in range(2):
            unfold[r, 64 + 32 * j + r // 4] = 0.5
        for j in range(4):
            unfold[r, 128 + 16 * j + r // 8] = 2.0**-1.5
        unfold[r, 192 + r // 16] = 0.25
    last = np.zeros((128, 256), np.float32)
    for r in range(128):
        last[r, r // 2] = ROOT_HALF
    wide = np.zeros((128, 256), np.float32)
    wide[:, :128] = pool
    wide[:, 128:] = pool.T
    halves = np.concatenate([wide, stage, fold, spread, unfold, last], axis=0)
    ancestor = np.where(pool.T > 0, 0.0, LOW)
    row_scale = np.where(level_of < 8, 2.0 ** (-level_of / 2.0), 0.0)[:, None] * np.ones((1, 128))
    diag = np.eye(128)
    near = np.full((64, 256), LOW)
    for r in range(64):
        for k in range(192):
            if level_of[64 + r] == 2 + k // 64:
                near[r, k] = 0.0
    far = np.full((16, 256), LOW)
    for r in range(16):
        for k in range(192):
            if level_of[112 + r] == 5 + k // 64:
                far[r, k] = 0.0
    singles = np.concatenate(
        [
            np.concatenate([ancestor, row_scale], axis=1),
            np.concatenate([diag, stage_scale[:, None] * np.ones((1, 128))], axis=1),
            near,
            far,
        ],
        axis=0,
    )
    return halves.astype(np.float32), singles.astype(np.float32)


T_POOL, T_STAGE, T_FOLD, T_SPREAD, T_UNFOLD, T_LAST = 0, 128, 256, 320, 512, 640
T_ROWS = 768
S_ANC, S_DIAG, S_NEAR, S_FAR = 0, 128, 256, 320
S_ROWS = 336
GROUP_AT = (0, 64, 128)
COPIES = 48


def mm(a, b):
    return lax.dot_general(a, b, (((1,), (0,)), ((), ())), preferred_element_type=F32)


def mm_nt(a, b):
    return lax.dot_general(a, b, (((1,), (1,)), ((), ())), preferred_element_type=F32)


def mm_tn(a, b):
    return lax.dot_general(a, b, (((0,), (0,)), ((), ())), preferred_element_type=F32)


def flipped(index, mask):
    for bit in range(8):
        if mask >> bit & 1:
            own = lax.rem(lax.div(index, 1 << bit), 2)
            index = index + (1 << bit) * (1 - 2 * own)
    return index


def kernel(
    heads,
    unroll,
    key_hbm, value_hbm, query_hbm, grad_hbm, half_hbm, single_hbm,
    att_hbm, dquery_hbm, dkey_hbm, dvalue_hbm,
    half_tab, single_tab, rows_in, level_one, coarse_q,
    stage_src, stage_recv,
    local_scores, local_dprob, expo_one, expo_near, expo_far, numer, tops, totals,
    att_buf, dquery_buf, dkv_buf, local_ds, local_probs, adjoint, offset, dcoarse_q, dlocal_kv,
    part_grad, swap_grad, send_grad, recv_grad, one_part, one_send, one_recv, plane_grad, chip_grad,
    load_sem, store_sem, send_sem, recv_sem,
):
    seq = lax.axis_index("seq")
    head = lax.axis_index("head")
    width = heads * DH
    core = lax.rem(seq, 2)
    other = 1 - core
    mate = (seq, 1 - head)
    twin = (flipped(seq, 1), head)
    near_dev = {n: (flipped(seq, n << 1), head) for n, _, _, _ in PARTNERS}
    far_dev = {n: (flipped(seq, n << 4), head) for n, _, _, _ in PARTNERS}
    mine = pl.ds(pl.multiple_of(head * width, width), width)
    theirs = pl.ds(pl.multiple_of((1 - head) * width, width), width)
    sources = (key_hbm, value_hbm, query_hbm, grad_hbm)

    def remote(src, dst, slot, device):
        return pltpu.make_async_remote_copy(
            src_ref=src, dst_ref=dst, send_sem=send_sem.at[slot], recv_sem=recv_sem.at[slot],
            device_id=device, device_id_type=MESH,
        )

    loads = [
        pltpu.make_async_copy(ref.at[:, mine], rows_in.at[i, pl.ds(0, 64)], load_sem.at[i])
        for i, ref in enumerate(sources)
    ]
    table_loads = [
        pltpu.make_async_copy(half_hbm, half_tab, load_sem.at[4]),
        pltpu.make_async_copy(single_hbm, single_tab, load_sem.at[5]),
    ]
    entry = [
        remote(ref.at[:, theirs], rows_in.at[i, pl.ds(64, 64)], i, mate)
        for i, ref in enumerate(sources)
    ]
    own_rows = pl.ds(pl.multiple_of(core * 64, 64), 64)
    twin_rows = pl.ds(pl.multiple_of(other * 64, 64), 64)
    one_swap = [
        remote(level_one.at[kv, own_rows], level_one.at[kv, own_rows], 4 + kv, twin) for kv in (0, 1)
    ]
    one_wait = [
        remote(level_one.at[kv, twin_rows], level_one.at[kv, twin_rows], 4 + kv, twin) for kv in (0, 1)
    ]

    def stage_copies(which, base, devices):
        return {
            n: remote(
                stage_src.at[which, pl.ds(src, count)],
                stage_recv.at[which, core, pl.ds(dst, count)],
                base + n, devices[n],
            )
            for n, src, dst, count in PARTNERS
        }

    def stage_shares(which, base):
        give = [
            remote(
                stage_recv.at[which, core, pl.ds(64 * i, 64)],
                stage_recv.at[which, core, pl.ds(64 * i, 64)], base + i, twin,
            )
            for i in range(3)
        ]
        take = [
            remote(
                stage_recv.at[which, other, pl.ds(64 * i, 64)],
                stage_recv.at[which, other, pl.ds(64 * i, 64)], base + i, twin,
            )
            for i in range(3)
        ]
        return give, take

    near_copies = stage_copies(0, 5, near_dev)
    far_copies = stage_copies(1, 12, far_dev)
    near_give, near_take = stage_shares(0, 20)
    far_give, far_take = stage_shares(1, 23)
    part_swap = [
        remote(part_grad.at[w, other], swap_grad.at[w], 26 + w, twin) for w in (0, 1)
    ]

    def grad_copies(which, base, devices):
        return {
            n: remote(
                send_grad.at[which, pl.ds(dst, count)],
                recv_grad.at[which, pl.ds(dst, count)],
                base + n, devices[n],
            )
            for n, _, dst, count in PARTNERS
        }

    near_back = grad_copies(0, 27, near_dev)
    far_back = grad_copies(1, 34, far_dev)
    one_back_early = remote(one_part.at[other], one_recv.at[other], 42, twin)
    one_take_early = remote(one_part.at[core], one_recv.at[core], 42, twin)
    one_back_late = remote(one_send, one_recv.at[core], 43, twin)
    one_take_late = remote(one_send, one_recv.at[other], 43, twin)
    results = ((att_buf, att_hbm), (dquery_buf, dquery_hbm), (dkv_buf.at[0], dkey_hbm), (dkv_buf.at[1], dvalue_hbm))
    stores = [
        pltpu.make_async_copy(buf.at[pl.ds(0, 64)], out.at[:, mine], store_sem.at[i])
        for i, (buf, out) in enumerate(results)
    ]
    exits = [
        remote(buf.at[pl.ds(64, 64)], out.at[:, mine], 44 + i, mate)
        for i, (buf, out) in enumerate(results)
    ]
    exit_waits = [
        remote(buf.at[pl.ds(64, 64)], out.at[:, theirs], 44 + i, mate)
        for i, (buf, out) in enumerate(results)
    ]

    for copy in loads + table_loads:
        copy.start()
    barrier = pltpu.get_barrier_semaphore()
    partners = [mate, twin] + list(near_dev.values()) + list(far_dev.values())
    for device in partners:
        pl.semaphore_signal(barrier, inc=1, device_id=device, device_id_type=MESH)
    pl.semaphore_wait(barrier, len(partners))
    for copy in entry:
        copy.start()

    def columns(h):
        return pl.ds(pl.multiple_of(h * DH, DH), DH)

    def each_head(*steps):
        def body(i, carry):
            for step in steps:
                for j in range(unroll):
                    step(i * unroll + j)
            return carry

        lax.fori_loop(0, heads // unroll, body, 0)

    for copy in table_loads:
        copy.wait()

    for kv in (0, 1):
        loads[kv].wait()
        entry[kv].wait_recv()

        def pool_one(h):
            cols = columns(h)
            pooled = mm(half_tab[pl.ds(T_POOL, 64), pl.ds(0, 128)], rows_in[kv, :, cols]) * ROOT_HALF
            level_one[kv, own_rows, cols] = pooled.astype(BF16)

        each_head(pool_one)
        one_swap[kv].start()

    loads[2].wait()
    entry[2].wait_recv()

    def pool_queries(h):
        cols = columns(h)
        pooled = mm(half_tab[pl.ds(T_POOL, 128), pl.ds(0, 128)], rows_in[2, :, cols])
        coarse_q[:, cols] = (pooled * single_tab[pl.ds(S_ANC, 128), pl.ds(128, 128)]).astype(BF16)

    each_head(pool_queries)

    for kv in (0, 1):
        one_wait[kv].wait_recv()

    def pool_near(h):
        cols = columns(h)
        pooled = mm(half_tab[pl.ds(T_POOL, 112), pl.ds(0, 128)], level_one[core, :, cols])
        pooled = (pooled * single_tab[pl.ds(S_ANC, 112), pl.ds(128, 128)]).astype(BF16)
        stage_src[0, :, cols] = pooled
        stage_recv[0, core, pl.ds(192, 16), cols] = pooled[96:112]

    each_head(pool_near)
    for copy in near_copies.values():
        copy.start()

    loads[3].wait()
    entry[3].wait_recv()

    def score_local(h):
        cols = columns(h)
        local_scores[h] = mm_nt(rows_in[2, :, cols], rows_in[0, :, cols]) * SCALE
        local_dprob[h] = mm_nt(rows_in[3, :, cols], rows_in[1, :, cols])

    def to_row(column, start, low, count):
        picked = column[low : low + count] * single_tab[pl.ds(S_DIAG + start + low, count), pl.ds(0, 128)]
        return jnp.sum(picked, axis=0, keepdims=True)

    def coarse_forward(h, group, start, rows, low, count, keys, vals, mask, expo):
        cols = columns(h)
        scores = mm_nt(coarse_q[pl.ds(start, rows), cols], keys) * SCALE
        if mask is not None:
            scores = scores + mask
        top = jnp.maximum(jnp.max(scores, axis=1, keepdims=True), FLOOR)
        weights = jnp.exp(scores - top)
        total = jnp.sum(weights, axis=1, keepdims=True)
        expo[h] = weights
        numer[h, pl.ds(GROUP_AT[group], rows)] = mm(weights.astype(BF16), vals)
        tops[h, pl.ds(group, 1)] = to_row(top, start, low, count)
        totals[h, pl.ds(group, 1)] = to_row(total, start, low, count)

    def forward_one(h):
        cols = columns(h)
        coarse_forward(
            h, 0, 0, 64, 0, 64, level_one[0, twin_rows, cols], level_one[1, twin_rows, cols], None, expo_one
        )

    def forward_near(h):
        cols = columns(h)
        coarse_forward(
            h, 1, 64, 64, 0, 56, stage_recv[0, 0, pl.ds(0, 192), cols], stage_recv[0, 1, pl.ds(0, 192), cols],
            single_tab[pl.ds(S_NEAR, 64), pl.ds(0, 192)], expo_near,
        )

    def forward_far(h):
        cols = columns(h)
        coarse_forward(
            h, 2, 112, 16, 8, 8, stage_recv[1, 0, pl.ds(0, 192), cols], stage_recv[1, 1, pl.ds(0, 192), cols],
            single_tab[pl.ds(S_FAR, 16), pl.ds(0, 192)], expo_far,
        )

    each_head(score_local)
    each_head(forward_one)

    for i, group in enumerate(((1,), (2, 3), (4, 5, 6, 7))):
        for n in group:
            near_copies[n].wait_recv()
        near_give[i].start()

    def pool_far(h):
        cols = columns(h)
        pooled = mm(half_tab[pl.ds(T_STAGE, 112), pl.ds(0, 208)], stage_recv[0, core, :, cols])
        pooled = pooled * single_tab[pl.ds(S_DIAG, 112), pl.ds(128, 128)]
        stage_src[1, :, cols] = pooled.astype(BF16)

    each_head(pool_far)
    for copy in far_copies.values():
        copy.start()
    for copy in near_take:
        copy.wait_recv()
    each_head(forward_near)

    for i, group in enumerate(((1,), (2, 3), (4, 5, 6, 7))):
        for n in group:
            far_copies[n].wait_recv()
        far_give[i].start()
    for copy in far_take:
        copy.wait_recv()
    each_head(forward_far)

    def combine(h):
        cols = columns(h)
        top_row = tops[h, pl.ds(0, 1)] + tops[h, pl.ds(1, 1)] + tops[h, pl.ds(2, 1)]
        total_row = totals[h, pl.ds(0, 1)] + totals[h, pl.ds(1, 1)] + totals[h, pl.ds(2, 1)]
        scores = local_scores[h]
        coarse = single_tab[pl.ds(S_ANC, 128), pl.ds(0, 128)] + top_row
        top = jnp.max(jnp.maximum(scores, coarse), axis=1, keepdims=True)
        expo = jnp.exp(scores - top)
        factor = jnp.exp(coarse - top)
        total = jnp.sum(expo + factor * total_row, axis=1, keepdims=True)
        inverse = 1.0 / total
        numer_all = jnp.concatenate(
            [
                numer[h, pl.ds(0, 112)],
                numer[h, pl.ds(112, 16)] + numer[h, pl.ds(128, 16)],
            ],
            axis=0,
        ).astype(BF16)
        outcome = (mm(expo.astype(BF16), rows_in[1, :, cols]) + mm(factor.astype(BF16), numer_all)) * inverse
        att_buf[:, cols] = outcome.astype(BF16)
        grad = rows_in[3, :, cols]
        dots = jnp.sum(grad.astype(F32) * outcome, axis=1, keepdims=True)
        probs = expo * inverse
        weight = (factor * inverse).astype(BF16)
        local_probs[h] = probs.astype(BF16)
        local_ds[h] = (probs * (local_dprob[h] - dots)).astype(BF16)
        adjoint[h] = mm_tn(weight, grad).astype(BF16)
        dots_wide = jnp.broadcast_to(dots, (128, 128))
        dots_high = dots_wide.astype(BF16)
        dots_low = (dots_wide - dots_high.astype(F32)).astype(BF16)
        offset[h] = mm_tn(weight, dots_high) + mm_tn(weight, dots_low)

    each_head(combine)

    def coarse_backward(h, start, rows, keys, vals, expo, dcoarse_at, put_key, put_value):
        cols = columns(h)
        weights = expo[h]
        adj = adjoint[h, pl.ds(start, rows)]
        inner = mm_nt(adj, vals) - offset[h, pl.ds(start, rows), pl.ds(0, 1)]
        dscore = (weights * inner).astype(BF16)
        dcoarse_q[h, pl.ds(dcoarse_at, rows)] = mm(dscore, keys)
        put_key((mm_tn(dscore, coarse_q[pl.ds(start, rows), cols]) * SCALE).astype(BF16))
        put_value(mm_tn(weights.astype(BF16), adj).astype(BF16))

    def backward_far(h):
        cols = columns(h)

        def put_key(x):
            part_grad[1, 0, :, cols] = x

        def put_value(x):
            part_grad[1, 1, :, cols] = x

        coarse_backward(
            h, 112, 16, stage_recv[1, 0, pl.ds(0, 192), cols], stage_recv[1, 1, pl.ds(0, 192), cols],
            expo_far, GROUP_AT[2], put_key, put_value,
        )

    def backward_near(h):
        cols = columns(h)

        def put_key(x):
            part_grad[0, 0, :, cols] = x

        def put_value(x):
            part_grad[0, 1, :, cols] = x

        coarse_backward(
            h, 64, 64, stage_recv[0, 0, pl.ds(0, 192), cols], stage_recv[0, 1, pl.ds(0, 192), cols],
            expo_near, GROUP_AT[1], put_key, put_value,
        )

    def backward_one(h):
        cols = columns(h)

        def put_key(x):
            one_part[0, :, cols] = x

        def put_value(x):
            one_part[1, :, cols] = x

        coarse_backward(
            h, 0, 64, level_one[0, twin_rows, cols], level_one[1, twin_rows, cols],
            expo_one, GROUP_AT[0], put_key, put_value,
        )

    each_head(backward_far)
    part_swap[1].start()
    stores[0].start()
    exits[0].start()
    each_head(backward_one)
    one_back_early.start()

    part_swap[1].wait_recv()

    def sum_far(h):
        cols = columns(h)
        both = part_grad[1, core, :, cols].astype(F32) + swap_grad[1, :, cols].astype(F32)
        send_grad[1, :, cols] = both.astype(BF16)

    each_head(sum_far)
    for copy in far_back.values():
        copy.start()

    each_head(backward_near)
    part_swap[0].start()

    def query_total(h):
        cols = columns(h)
        coarse = jnp.concatenate(
            [
                dcoarse_q[h, pl.ds(0, 112)],
                dcoarse_q[h, pl.ds(112, 16)] + dcoarse_q[h, pl.ds(128, 16)],
            ],
            axis=0,
        ) * single_tab[pl.ds(S_ANC, 128), pl.ds(128, 128)]
        total = mm(local_ds[h], rows_in[0, :, cols])
        total = total + mm(half_tab[pl.ds(T_POOL, 128), pl.ds(128, 128)], coarse.astype(BF16))
        dquery_buf[:, cols] = (total * SCALE).astype(BF16)

    each_head(query_total)
    stores[1].start()
    exits[1].start()

    def local_back(h):
        cols = columns(h)
        dlocal_kv[0, :, cols] = mm_tn(local_ds[h], rows_in[2, :, cols]) * SCALE
        dlocal_kv[1, :, cols] = mm_tn(local_probs[h], rows_in[3, :, cols])

    each_head(local_back)

    for copy in far_back.values():
        copy.wait_recv()
    part_swap[0].wait_recv()

    def sum_near(h):
        cols = columns(h)
        plane = mm(half_tab[pl.ds(T_FOLD, 64), pl.ds(0, 192)], recv_grad[1, :, cols]).astype(BF16)
        plane_grad[:, cols] = plane
        both = part_grad[0, core, :, cols].astype(F32) + swap_grad[0, :, cols].astype(F32)
        both = both + mm(half_tab[pl.ds(T_SPREAD, 192), pl.ds(0, 64)], plane)
        send_grad[0, :, cols] = both.astype(BF16)

    each_head(sum_near)
    for copy in near_back.values():
        copy.start()
    for copy in near_back.values():
        copy.wait_recv()

    def sum_one(h):
        cols = columns(h)
        chip = mm(half_tab[pl.ds(T_UNFOLD, 128), pl.ds(0, 192)], recv_grad[0, :, cols])
        chip = chip + mm(half_tab[pl.ds(T_UNFOLD, 128), pl.ds(192, 64)], plane_grad[:, cols])
        chip_grad[:, cols] = chip

    def sum_one_send(h):
        cols = columns(h)
        one_send[:, cols] = (one_part[core, :, cols].astype(F32) + chip_grad[twin_rows, cols]).astype(BF16)

    each_head(sum_one)
    each_head(sum_one_send)
    one_back_late.start()
    one_take_early.wait_recv()
    one_take_late.wait_recv()

    def finish(h):
        cols = columns(h)
        last = half_tab[pl.ds(T_LAST, 128), pl.ds(0, 64)]
        total = one_recv[core, :, cols].astype(F32) + chip_grad[own_rows, cols]
        dkv_buf[core, :, cols] = (dlocal_kv[core, :, cols] + mm(last, total.astype(BF16))).astype(BF16)
        dkv_buf[other, :, cols] = (dlocal_kv[other, :, cols] + mm(last, one_recv[other, :, cols])).astype(BF16)

    each_head(finish)
    for i in (2, 3):
        stores[i].start()
        exits[i].start()

    for copy in entry + one_swap + near_give + far_give + part_swap + [one_back_early, one_back_late] + exits:
        copy.wait_send()
    for group in (near_copies, far_copies, near_back, far_back):
        for copy in group.values():
            copy.wait_send()
    for copy in stores:
        copy.wait()
    for copy in exit_waits:
        copy.wait_recv()


def solution(mesh):
    halves, singles = tables()
    halves = halves.astype(BF16)
    unroll = 4

    def local(queries, key_rows, values, out_grad):
        rows, columns = queries.shape
        width = columns // 2
        heads = width // DH
        tall = 2 * rows
        anywhere = pl.BlockSpec(memory_space=pl.ANY)
        out = jax.ShapeDtypeStruct((rows, columns), BF16)
        vmem = pltpu.VMEM
        scratch = [
            vmem((T_ROWS, 256), BF16),
            vmem((S_ROWS, 256), F32),
            vmem((4, tall, width), BF16),
            vmem((2, 128, width), BF16),
            vmem((128, width), BF16),
            vmem((2, 112, width), BF16),
            vmem((2, 2, 208, width), BF16),
            vmem((heads, 128, 128), F32),
            vmem((heads, 128, 128), F32),
            vmem((heads, 64, 64), F32),
            vmem((heads, 64, 192), F32),
            vmem((heads, 16, 192), F32),
            vmem((heads, 144, 128), F32),
            vmem((heads, 8, 128), F32),
            vmem((heads, 8, 128), F32),
            vmem((tall, width), BF16),
            vmem((tall, width), BF16),
            vmem((2, tall, width), BF16),
            vmem((heads, 128, 128), BF16),
            vmem((heads, 128, 128), BF16),
            vmem((heads, 128, 128), BF16),
            vmem((heads, 128, 128), F32),
            vmem((heads, 144, 128), F32),
            vmem((2, tall, width), F32),
            vmem((2, 2, 192, width), BF16),
            vmem((2, 192, width), BF16),
            vmem((2, 192, width), BF16),
            vmem((2, 192, width), BF16),
            vmem((2, 64, width), BF16),
            vmem((64, width), BF16),
            vmem((2, 64, width), BF16),
            vmem((64, width), BF16),
            vmem((128, width), F32),
            pltpu.SemaphoreType.DMA((6,)),
            pltpu.SemaphoreType.DMA((4,)),
            pltpu.SemaphoreType.DMA((COPIES,)),
            pltpu.SemaphoreType.DMA((COPIES,)),
        ]
        return pl.pallas_call(
            functools.partial(kernel, heads, unroll),
            out_shape=(out,) * 4,
            in_specs=[anywhere] * 6,
            out_specs=(anywhere,) * 4,
            scratch_shapes=scratch,
            compiler_params=pltpu.CompilerParams(
                collective_id=0, has_side_effects=True, vmem_limit_bytes=60 << 20
            ),
            name="sibling_attention",
        )(key_rows, values, queries, out_grad, jnp.asarray(halves), jnp.asarray(singles))

    spec = P(("seq", "head"), None)
    return jax.shard_map(
        local, mesh=mesh, in_specs=(spec,) * 4, out_specs=(spec,) * 4, check_vma=False
    )
```

```python
import functools
import math

import jax
import jax.numpy as jnp
import numpy as np
from jax import lax
from jax.experimental import pallas as pl
from jax.experimental.pallas import tpu as pltpu
from jax.sharding import PartitionSpec as P

MESH = pl.DeviceIdType.MESH
BF16 = jnp.bfloat16
F32 = jnp.float32
DH = 128
SCALE = 1.0 / math.sqrt(DH)
LOW = -1e30
FLOOR = -1e29

NEAR = ((1, 64, 0, 32), (2, 96, 32, 16), (3, 96, 48, 16))
FAR = ((1, 0, 0, 64), (2, 64, 64, 32), (3, 64, 96, 32))
FAR += tuple((n, 96, 128 + 16 * (n - 4), 16) for n in (4, 5, 6, 7))
PLANE = 16


def tables():
    level_of = np.zeros(128, np.int64)
    pool = np.zeros((128, 128), np.float32)
    row = 0
    for level in range(1, 8):
        for i in range(128 >> level):
            pool[row, i << level : (i + 1) << level] = 1.0
            level_of[row] = level
            row += 1
    level_of[127] = 99
    wide = np.concatenate([pool, pool.T], axis=1)
    pick = np.zeros((2, 128, 256), np.float32)
    compact = np.zeros((2, 128, 256), np.float32)
    fold = np.zeros((128, 256), np.float32)
    for kv in range(2):
        for i in range(PLANE):
            for r in range(8):
                pick[kv, 8 * i + r, 16 * i + 8 * kv + r] = 1.0
            for r in range(4):
                compact[kv, 4 * i + r, 16 * i + 8 * kv + r] = 1.0
            for r in range(2):
                compact[kv, 64 + 2 * i + r, 16 * i + 8 * kv + 4 + r] = 1.0
            compact[kv, 96 + i, 16 * i + 8 * kv + 6] = 1.0
    for i in range(PLANE):
        for r in range(4):
            fold[8 * i + r, 4 * i + r] = 1.0
        for r in range(2):
            for j in range(2):
                fold[8 * i + 4 + r, 64 + 32 * j + 2 * i + r] = 1.0
        for j in range(4):
            fold[8 * i + 6, 128 + 16 * j + i] = 1.0
    halves = np.concatenate([wide, pick[0], pick[1], compact[0], compact[1], fold], axis=0)
    ancestor = np.where(pool.T > 0, 0.0, LOW)
    row_scale = np.where(level_of < 8, 2.0 ** (-level_of / 2.0), 0.0)[:, None] * np.ones((1, 128))
    shard = np.arange(128) // 8
    across = np.where(shard[:, None] // 8 != shard[None, :] // 8, 0.0, LOW)
    near = np.full((48, 256), LOW)
    for r in range(48):
        for k in range(128):
            if level_of[64 + r] == (2 if k % 64 < 32 else 3):
                near[r, k] = 0.0
    far = np.full((128, 256), LOW)
    for r in range(128):
        for k in range(192):
            if level_of[120 + r % 8] == 5 + k // 64:
                far[r, k] = 0.0
    singles = np.concatenate(
        [
            np.concatenate([ancestor, row_scale], axis=1),
            np.concatenate([np.eye(128), across], axis=1),
            near,
            far,
        ],
        axis=0,
    )
    return halves.astype(np.float32), singles.astype(np.float32)


T_POOL, T_PICK, T_COMPACT, T_FOLD = 0, 128, 384, 640
T_ROWS = 768
S_ANC, S_DIAG, S_NEAR, S_FAR = 0, 128, 256, 304
S_ROWS = 432

C_ENTRY, C_EXIT, C_ONE, C_SHARE, C_PART, C_ONE_BACK = 0, 4, 8, 9, 10, 11
C_NEAR, C_NEAR_BACK, C_FAR, C_FAR_BACK = 11, 14, 17, 24
C_ROWS, C_QUERY, C_SUMS, C_ADJ, C_DQUERY, C_DROWS = 32, 48, 64, 80, 96, 112
COPIES = 128


def mm(a, b):
    return lax.dot_general(a, b, (((1,), (0,)), ((), ())), preferred_element_type=F32)


def mm_nt(a, b):
    return lax.dot_general(a, b, (((1,), (1,)), ((), ())), preferred_element_type=F32)


def mm_tn(a, b):
    return lax.dot_general(a, b, (((0,), (0,)), ((), ())), preferred_element_type=F32)


def flipped(index, mask):
    for bit in range(8):
        if mask >> bit & 1:
            own = lax.rem(lax.div(index, 1 << bit), 2)
            index = index + (1 << bit) * (1 - 2 * own)
    return index


def kernel(
    heads,
    unroll,
    key_hbm, value_hbm, query_hbm, grad_hbm, half_hbm, single_hbm,
    att_hbm, dquery_hbm, dkey_hbm, dvalue_hbm,
    half_tab, single_tab, rows_in, coarse_kv, coarse_q, one_kv, near_kv,
    rows_send, rows_recv, query_send, query_recv, far_send, far_kv, pair_kv,
    local_scores, local_dprob, expo_one, expo_near, expo_far, numer, tops, totals,
    sums_send, sums_recv, adj_send, adj_recv, dquery_send, dquery_recv, drows_send, drows_recv,
    dfar_send, dfar_recv,
    att_buf, dquery_buf, dkv_buf, local_ds, local_probs, adjoint, offset, dcoarse_q, dlocal_kv,
    part_grad, swap_grad, send_grad, recv_grad, one_part, one_recv,
    load_sem, store_sem, self_sem, send_sem, recv_sem,
):
    seq = lax.axis_index("seq")
    head = lax.axis_index("head")
    width = heads * DH
    core = lax.rem(seq, 2)
    place = lax.rem(seq, PLANE)
    chip = lax.div(place, 2)
    mate = (seq, 1 - head)
    twin = (flipped(seq, 1), head)
    near_dev = {n: (flipped(seq, n << 1), head) for n, _, _, _ in NEAR}
    far_dev = {n: (flipped(seq, n << 4), head) for n, _, _, _ in FAR}
    peers = []
    for m in range(PLANE):
        there = flipped(seq, m)
        slot = lax.rem(there, PLANE)
        peers.append(((there, head), slot, lax.div(slot, 2), lax.rem(slot, 2)))
    mine = pl.ds(pl.multiple_of(head * width, width), width)
    theirs = pl.ds(pl.multiple_of((1 - head) * width, width), width)
    sources = (key_hbm, value_hbm, query_hbm, grad_hbm)

    def remote(src, dst, slot, device):
        return pltpu.make_async_remote_copy(
            src_ref=src, dst_ref=dst, send_sem=send_sem.at[slot], recv_sem=recv_sem.at[slot],
            device_id=device, device_id_type=MESH,
        )

    def slab(slot, rows):
        return pl.ds(pl.multiple_of(slot * rows, rows), rows)

    loads = [
        pltpu.make_async_copy(ref.at[:, mine], rows_in.at[i, pl.ds(0, 64)], load_sem.at[i])
        for i, ref in enumerate(sources)
    ]
    table_loads = [
        pltpu.make_async_copy(half_hbm, half_tab, load_sem.at[4]),
        pltpu.make_async_copy(single_hbm, single_tab, load_sem.at[5]),
    ]
    entry = [
        remote(ref.at[:, theirs], rows_in.at[i, pl.ds(64, 64)], C_ENTRY + i, mate)
        for i, ref in enumerate(sources)
    ]
    one_swap = remote(coarse_kv.at[:, pl.ds(0, 64)], one_kv, C_ONE, twin)
    near_copies = [
        remote(coarse_kv.at[:, pl.ds(src, count)], near_kv.at[0, :, pl.ds(dst, count)], C_NEAR + n, near_dev[n])
        for n, src, dst, count in NEAR
    ]
    share = remote(near_kv.at[0], near_kv.at[1], C_SHARE, twin)
    far_copies = [
        remote(far_send.at[pl.ds(src, count)], far_kv.at[pl.ds(dst, count)], C_FAR + n, far_dev[n])
        for n, src, dst, count in FAR
    ]
    far_back = [
        remote(dfar_send.at[pl.ds(dst, count)], dfar_recv.at[pl.ds(dst, count)], C_FAR_BACK + n, far_dev[n])
        for n, _, dst, count in FAR
    ]
    part_swap = remote(part_grad.at[1], swap_grad, C_PART, twin)
    near_back = [
        remote(send_grad.at[:, pl.ds(dst, count)], recv_grad.at[:, pl.ds(dst, count)], C_NEAR_BACK + n, near_dev[n])
        for n, _, dst, count in NEAR
    ]
    one_back = remote(one_part, one_recv, C_ONE_BACK, twin)

    class Spread:
        def __init__(self, which, base, send, recv, rows):
            self.local = pltpu.make_async_copy(
                send.at[chip, core], recv.at[slab(place, rows)], self_sem.at[which]
            )
            self.out = []
            self.come = []
            for m in range(1, PLANE):
                device, slot, owner, group = peers[m]
                self.out.append(remote(send.at[owner, group], recv.at[slab(place, rows)], base + m, device))
                self.come.append(remote(send.at[owner, group], recv.at[slab(slot, rows)], base + m, device))

        def start(self):
            for copy in self.out:
                copy.start()
            self.local.start()

        def wait_recv(self):
            self.local.wait()
            for copy in self.come:
                copy.wait_recv()

        def wait_send(self):
            for copy in self.out:
                copy.wait_send()

    class Return(Spread):
        def __init__(self, which, base, send, recv, rows):
            self.local = pltpu.make_async_copy(
                send.at[slab(place, rows)], recv.at[chip, core], self_sem.at[which]
            )
            self.out = []
            self.come = []
            for m in range(1, PLANE):
                device, slot, owner, group = peers[m]
                self.out.append(remote(send.at[slab(slot, rows)], recv.at[chip, core], base + m, device))
                self.come.append(remote(send.at[slab(slot, rows)], recv.at[owner, group], base + m, device))

    rows_out = Spread(0, C_ROWS, rows_send, rows_recv, 16)
    query_out = Spread(1, C_QUERY, query_send, query_recv, 8)
    sums_back = Return(2, C_SUMS, sums_send, sums_recv, 16)
    adj_out = Spread(3, C_ADJ, adj_send, adj_recv, 16)
    dquery_back = Return(4, C_DQUERY, dquery_send, dquery_recv, 8)
    drows_back = Return(5, C_DROWS, drows_send, drows_recv, 16)

    results = ((att_buf, att_hbm), (dquery_buf, dquery_hbm), (dkv_buf.at[0], dkey_hbm), (dkv_buf.at[1], dvalue_hbm))
    stores = [
        pltpu.make_async_copy(buf.at[pl.ds(0, 64)], out.at[:, mine], store_sem.at[i])
        for i, (buf, out) in enumerate(results)
    ]
    exits = [
        remote(buf.at[pl.ds(64, 64)], out.at[:, mine], C_EXIT + i, mate)
        for i, (buf, out) in enumerate(results)
    ]
    exit_waits = [
        remote(buf.at[pl.ds(64, 64)], out.at[:, theirs], C_EXIT + i, mate)
        for i, (buf, out) in enumerate(results)
    ]

    for copy in loads + table_loads:
        copy.start()
    barrier = pltpu.get_barrier_semaphore()
    partners = [mate] + [peer[0] for peer in peers[1:]] + list(far_dev.values())
    for device in partners:
        pl.semaphore_signal(barrier, inc=1, device_id=device, device_id_type=MESH)
    pl.semaphore_wait(barrier, len(partners))
    for copy in entry:
        copy.start()

    def columns(h):
        return pl.ds(pl.multiple_of(h * DH, DH), DH)

    def each_head(*steps):
        def body(i, carry):
            for step in steps:
                for j in range(unroll):
                    step(i * unroll + j)
            return carry

        lax.fori_loop(0, heads // unroll, body, 0)

    for copy in table_loads:
        copy.wait()
    everything = pl.ds(0, 128)
    right = pl.ds(128, 128)

    def pooled(which, h):
        rows = mm(half_tab[pl.ds(T_POOL, 128), pl.ds(0, 128)], rows_in[which, :, columns(h)])
        return rows * single_tab[pl.ds(S_ANC, 128), right]

    for kv in (0, 1):
        loads[kv].wait()
        entry[kv].wait_recv()

    def pool_rows(h):
        cols = columns(h)
        keys = pooled(0, h)
        vals = pooled(1, h)
        coarse_kv[0, :, cols] = keys.astype(BF16)
        coarse_kv[1, :, cols] = vals.astype(BF16)
        for group in (0, 1):
            low = 112 + 8 * group
            both = jnp.concatenate([keys[low : low + 8], vals[low : low + 8]], axis=0)
            rows_send[h, group] = both.astype(BF16)

    each_head(pool_rows)
    rows_out.start()
    for copy in near_copies:
        copy.start()
    one_swap.start()

    loads[2].wait()
    entry[2].wait_recv()

    def pool_queries(h):
        rows = pooled(2, h)
        short = rows.astype(BF16)
        coarse_q[:, columns(h)] = short
        for group in (0, 1):
            query_send[h, group] = short.astype(F32)[112 + 8 * group : 120 + 8 * group]

    each_head(pool_queries)
    query_out.start()

    rows_out.wait_recv()

    @pl.when(core == 1)
    def _():
        for kv in (0, 1):
            rows = mm(half_tab[pl.ds(T_COMPACT + 128 * kv, 112)], rows_recv[...])
            far_send[:, pl.ds(128 * kv, 128)] = rows.astype(BF16)
        for copy in far_copies:
            copy.start()

    @pl.when(core == 0)
    def _():
        for kv in (0, 1):
            rows = mm(half_tab[pl.ds(T_PICK + 128 * kv, 128)], rows_recv[...])
            pair_kv[:, pl.ds(128 * kv, 128)] = rows.astype(BF16)

    def to_row(column, start):
        count = column.shape[0]
        picked = column * single_tab[pl.ds(S_DIAG + start, count), everything]
        return jnp.sum(picked, axis=0, keepdims=True)

    def attend(queries, keys, vals, mask):
        scores = mm_nt(queries, keys) * SCALE
        if mask is not None:
            scores = scores + mask
        top = jnp.maximum(jnp.max(scores, axis=1, keepdims=True), FLOOR)
        weights = jnp.exp(scores - top)
        total = jnp.sum(weights, axis=1, keepdims=True)
        return weights, top, total, mm(weights.astype(BF16), vals)

    def attend_back(weights, adj, shift, queries, keys, vals):
        inner = mm_nt(adj, vals) - shift
        dscore = (weights * inner).astype(BF16)
        dkeys = mm_tn(dscore, queries) * SCALE
        return mm(dscore, keys), dkeys, mm_tn(weights.astype(BF16), adj)

    def near_rows(kv, h):
        return jnp.concatenate([near_kv[0, kv, :, columns(h)], near_kv[1, kv, :, columns(h)]], axis=0)

    def forward_one(h):
        cols = columns(h)
        weights, top, total, sums = attend(
            coarse_q[pl.ds(0, 64), cols], one_kv[0, :, cols], one_kv[1, :, cols], None
        )
        expo_one[h] = weights
        numer[h, pl.ds(0, 64)] = sums
        tops[h, pl.ds(0, 1)] = to_row(top, 0)
        totals[h, pl.ds(0, 1)] = to_row(total, 0)

    def forward_near(h):
        weights, top, total, sums = attend(
            coarse_q[pl.ds(64, 48), columns(h)], near_rows(0, h), near_rows(1, h),
            single_tab[pl.ds(S_NEAR, 48), everything],
        )
        expo_near[h] = weights
        numer[h, pl.ds(64, 48)] = sums
        tops[h, pl.ds(1, 1)] = to_row(top, 64)
        totals[h, pl.ds(1, 1)] = to_row(total, 64)

    one_swap.wait_recv()
    each_head(forward_one)
    for copy in near_copies:
        copy.wait_recv()
    share.start()

    query_out.wait_recv()

    def forward_far(keys, vals, mask, span):
        weights, top, total, sums = attend(query_recv[...].astype(BF16), keys, vals, mask)
        expo_far[:, pl.ds(0, span)] = weights
        lanes = lax.broadcasted_iota(jnp.int32, (128, 128), 1)
        pair = jnp.where(lanes < 64, top, total)
        whole = jnp.concatenate([sums.reshape(PLANE, 8, 128), pair.reshape(PLANE, 8, 128)], axis=1)
        sums_send[...] = whole.reshape(PLANE * 16, 128)

    @pl.when(core == 0)
    def _():
        forward_far(
            pair_kv[:, everything], pair_kv[:, right], single_tab[pl.ds(S_DIAG, 128), right], 128
        )

    @pl.when(core == 1)
    def _():
        for copy in far_copies:
            copy.wait_recv()
        forward_far(
            far_kv[:, everything], far_kv[:, right], single_tab[pl.ds(S_FAR, 128), pl.ds(0, 192)], 192
        )

    sums_back.start()

    loads[3].wait()
    entry[3].wait_recv()

    def score_local(h):
        cols = columns(h)
        local_scores[h] = mm_nt(rows_in[2, :, cols], rows_in[0, :, cols]) * SCALE
        local_dprob[h] = mm_nt(rows_in[3, :, cols], rows_in[1, :, cols])

    each_head(score_local)
    share.wait_recv()
    each_head(forward_near)
    sums_back.wait_recv()

    def combine(h):
        cols = columns(h)
        top_row = tops[h, pl.ds(0, 1)] + tops[h, pl.ds(1, 1)]
        total_row = totals[h, pl.ds(0, 1)] + totals[h, pl.ds(1, 1)]
        for group in (0, 1):
            top_row = top_row + to_row(sums_recv[h, group, pl.ds(8, 8), pl.ds(0, 1)], 112 + 8 * group)
            total_row = total_row + to_row(sums_recv[h, group, pl.ds(8, 8), pl.ds(64, 1)], 112 + 8 * group)
        scores = local_scores[h]
        coarse = single_tab[pl.ds(S_ANC, 128), everything] + top_row
        top = jnp.max(jnp.maximum(scores, coarse), axis=1, keepdims=True)
        expo = jnp.exp(scores - top)
        factor = jnp.exp(coarse - top)
        total = jnp.sum(expo + factor * total_row, axis=1, keepdims=True)
        inverse = 1.0 / total
        numer_all = jnp.concatenate(
            [numer[h], sums_recv[h, 0, pl.ds(0, 8)], sums_recv[h, 1, pl.ds(0, 8)]], axis=0
        ).astype(BF16)
        outcome = (mm(expo.astype(BF16), rows_in[1, :, cols]) + mm(factor.astype(BF16), numer_all)) * inverse
        att_buf[:, cols] = outcome.astype(BF16)
        grad = rows_in[3, :, cols]
        dots = jnp.sum(grad.astype(F32) * outcome, axis=1, keepdims=True)
        probs = expo * inverse
        weight = (factor * inverse).astype(BF16)
        local_probs[h] = probs.astype(BF16)
        local_ds[h] = (probs * (local_dprob[h] - dots)).astype(BF16)
        adj = mm_tn(weight, grad)
        adjoint[h] = adj.astype(BF16)
        dots_wide = jnp.broadcast_to(dots, (128, 128))
        dots_high = dots_wide.astype(BF16)
        dots_low = (dots_wide - dots_high.astype(F32)).astype(BF16)
        shift = mm_tn(weight, dots_high) + mm_tn(weight, dots_low)
        offset[h] = shift
        for group in (0, 1):
            low = 112 + 8 * group
            adj_send[h, group, pl.ds(0, 8)] = adj[low : low + 8]
            adj_send[h, group, pl.ds(8, 8)] = shift[low : low + 8]

    each_head(combine)
    adj_out.start()
    stores[0].start()
    exits[0].start()

    def backward_near(h):
        cols = columns(h)
        dqueries, dkeys, dvals = attend_back(
            expo_near[h], adjoint[h, pl.ds(64, 48)], offset[h, pl.ds(64, 48), pl.ds(0, 1)],
            coarse_q[pl.ds(64, 48), cols], near_rows(0, h), near_rows(1, h),
        )
        dcoarse_q[h, pl.ds(64, 48)] = dqueries
        for side in (0, 1):
            part_grad[side, 0, :, cols] = dkeys[64 * side : 64 * side + 64].astype(BF16)
            part_grad[side, 1, :, cols] = dvals[64 * side : 64 * side + 64].astype(BF16)

    def backward_one(h):
        cols = columns(h)
        dqueries, dkeys, dvals = attend_back(
            expo_one[h], adjoint[h, pl.ds(0, 64)], offset[h, pl.ds(0, 64), pl.ds(0, 1)],
            coarse_q[pl.ds(0, 64), cols], one_kv[0, :, cols], one_kv[1, :, cols],
        )
        dcoarse_q[h, pl.ds(0, 64)] = dqueries
        one_part[0, :, cols] = dkeys.astype(BF16)
        one_part[1, :, cols] = dvals.astype(BF16)

    each_head(backward_near)
    part_swap.start()
    adj_out.wait_recv()

    def backward_far(keys, vals, span):
        arrived = adj_recv[...].reshape(PLANE, 16, 128)
        adj = arrived[:, 0:8].reshape(128, 128).astype(BF16)
        shift = arrived[:, 8:16].reshape(128, 128)[:, 0:1]
        return attend_back(
            expo_far[:, pl.ds(0, span)], adj, shift, query_recv[...].astype(BF16), keys, vals
        )

    def put_rows(dkeys, dvals):
        whole = jnp.concatenate([dkeys.reshape(PLANE, 8, 128), dvals.reshape(PLANE, 8, 128)], axis=1)
        drows_send[...] = whole.reshape(PLANE * 16, 128)

    @pl.when(core == 0)
    def _():
        dqueries, dkeys, dvals = backward_far(pair_kv[:, everything], pair_kv[:, right], 128)
        dquery_send[...] = dqueries
        put_rows(dkeys, dvals)

    @pl.when(core == 1)
    def _():
        dqueries, dkeys, dvals = backward_far(far_kv[:, everything], far_kv[:, right], 192)
        dquery_send[...] = dqueries
        dfar_send[:, everything] = dkeys.astype(BF16)
        dfar_send[:, right] = dvals.astype(BF16)
        for copy in far_back:
            copy.start()

    dquery_back.start()

    @pl.when(core == 0)
    def _():
        for copy in drows_back.out:
            copy.start()
        drows_back.local.start()

    part_swap.wait_recv()

    def sum_near(h):
        cols = columns(h)
        for kv in (0, 1):
            both = part_grad[0, kv, :, cols].astype(F32) + swap_grad[kv, :, cols].astype(F32)
            send_grad[kv, :, cols] = both.astype(BF16)

    each_head(sum_near)
    for copy in near_back:
        copy.start()
    each_head(backward_one)
    one_back.start()

    @pl.when(core == 1)
    def _():
        for copy in far_back:
            copy.wait_recv()
        both = mm(half_tab[pl.ds(T_FOLD, 128), pl.ds(0, 192)], dfar_recv[...])
        put_rows(both[:, 0:128], both[:, 128:256])
        for copy in drows_back.out:
            copy.start()
        drows_back.local.start()

    dquery_back.wait_recv()

    def unpooled(rows):
        scaled = rows * single_tab[pl.ds(S_ANC, 128), right]
        return mm(half_tab[pl.ds(T_POOL, 128), right], scaled.astype(BF16))

    def query_total(h):
        cols = columns(h)
        coarse = jnp.concatenate([dcoarse_q[h], dquery_recv[h, 0], dquery_recv[h, 1]], axis=0)
        total = mm(local_ds[h], rows_in[0, :, cols]) + unpooled(coarse)
        dquery_buf[:, cols] = (total * SCALE).astype(BF16)

    each_head(query_total)
    stores[1].start()
    exits[1].start()

    def local_back(h):
        cols = columns(h)
        dlocal_kv[0, :, cols] = mm_tn(local_ds[h], rows_in[2, :, cols]) * SCALE
        dlocal_kv[1, :, cols] = mm_tn(local_probs[h], rows_in[3, :, cols])

    each_head(local_back)
    one_back.wait_recv()
    for copy in near_back:
        copy.wait_recv()
    drows_back.wait_recv()

    def finish(kv):
        def step(h):
            cols = columns(h)
            coarse = jnp.concatenate(
                [
                    one_recv[kv, :, cols].astype(F32),
                    recv_grad[kv, pl.ds(0, 32), cols].astype(F32),
                    recv_grad[kv, pl.ds(32, 16), cols].astype(F32)
                    + recv_grad[kv, pl.ds(48, 16), cols].astype(F32),
                    drows_recv[h, 0, pl.ds(8 * kv, 8)],
                    drows_recv[h, 1, pl.ds(8 * kv, 8)],
                ],
                axis=0,
            )
            dkv_buf[kv, :, cols] = (dlocal_kv[kv, :, cols] + unpooled(coarse)).astype(BF16)

        return step

    for kv in (0, 1):
        each_head(finish(kv))
        stores[2 + kv].start()
        exits[2 + kv].start()

    for copy in entry + near_copies + near_back + [one_swap, share, part_swap, one_back] + exits:
        copy.wait_send()
    for copy in (rows_out, query_out, sums_back, adj_out, dquery_back, drows_back):
        copy.wait_send()

    @pl.when(core == 1)
    def _():
        for copy in far_copies + far_back:
            copy.wait_send()

    for copy in stores:
        copy.wait()
    for copy in exit_waits:
        copy.wait_recv()


def solution(mesh):
    halves, singles = tables()
    halves = halves.astype(BF16)
    unroll = 4

    def local(queries, key_rows, values, out_grad):
        rows, columns = queries.shape
        width = columns // 2
        heads = width // DH
        tall = 2 * rows
        anywhere = pl.BlockSpec(memory_space=pl.ANY)
        out = jax.ShapeDtypeStruct((rows, columns), BF16)
        vmem = pltpu.VMEM
        scratch = [
            vmem((T_ROWS, 256), BF16),
            vmem((S_ROWS, 256), F32),
            vmem((4, tall, width), BF16),
            vmem((2, 128, width), BF16),
            vmem((128, width), BF16),
            vmem((2, 64, width), BF16),
            vmem((2, 2, 64, width), BF16),
            vmem((heads, 2, 16, 128), BF16),
            vmem((PLANE * 16, 128), BF16),
            vmem((heads, 2, 8, 128), F32),
            vmem((PLANE * 8, 128), F32),
            vmem((112, 256), BF16),
            vmem((192, 256), BF16),
            vmem((128, 256), BF16),
            vmem((heads, 128, 128), F32),
            vmem((heads, 128, 128), F32),
            vmem((heads, 64, 64), F32),
            vmem((heads, 48, 128), F32),
            vmem((128, 192), F32),
            vmem((heads, 112, 128), F32),
            vmem((heads, 8, 128), F32),
            vmem((heads, 8, 128), F32),
            vmem((PLANE * 16, 128), F32),
            vmem((heads, 2, 16, 128), F32),
            vmem((heads, 2, 16, 128), F32),
            vmem((PLANE * 16, 128), F32),
            vmem((PLANE * 8, 128), F32),
            vmem((heads, 2, 8, 128), F32),
            vmem((PLANE * 16, 128), F32),
            vmem((heads, 2, 16, 128), F32),
            vmem((192, 256), BF16),
            vmem((192, 256), BF16),
            vmem((tall, width), BF16),
            vmem((tall, width), BF16),
            vmem((2, tall, width), BF16),
            vmem((heads, 128, 128), BF16),
            vmem((heads, 128, 128), BF16),
            vmem((heads, 128, 128), BF16),
            vmem((heads, 128, 128), F32),
            vmem((heads, 112, 128), F32),
            vmem((2, tall, width), F32),
            vmem((2, 2, 64, width), BF16),
            vmem((2, 64, width), BF16),
            vmem((2, 64, width), BF16),
            vmem((2, 64, width), BF16),
            vmem((2, 64, width), BF16),
            vmem((2, 64, width), BF16),
            pltpu.SemaphoreType.DMA((6,)),
            pltpu.SemaphoreType.DMA((4,)),
            pltpu.SemaphoreType.DMA((6,)),
            pltpu.SemaphoreType.DMA((COPIES,)),
            pltpu.SemaphoreType.DMA((COPIES,)),
        ]
        return pl.pallas_call(
            functools.partial(kernel, heads, unroll),
            out_shape=(out,) * 4,
            in_specs=[anywhere] * 6,
            out_specs=(anywhere,) * 4,
            scratch_shapes=scratch,
            compiler_params=pltpu.CompilerParams(
                collective_id=0, has_side_effects=True, vmem_limit_bytes=60 << 20
            ),
            name="sibling_attention",
        )(key_rows, values, queries, out_grad, jnp.asarray(halves), jnp.asarray(singles))

    spec = P(("seq", "head"), None)
    return jax.shard_map(
        local, mesh=mesh, in_specs=(spec,) * 4, out_specs=(spec,) * 4, check_vma=False
    )
```

```python
import functools
import math

import jax
import jax.numpy as jnp
import numpy as np
from jax import lax
from jax.experimental import pallas as pl
from jax.experimental.pallas import tpu as pltpu
from jax.sharding import PartitionSpec as P

MESH = pl.DeviceIdType.MESH
BF16 = jnp.bfloat16
F32 = jnp.float32
DH = 128
SCALE = 1.0 / math.sqrt(DH)
LOW = -1e30
FLOOR = -1e29

NEAR = ((1, 64, 0, 32), (2, 96, 32, 16), (3, 96, 48, 16))
FAR = ((1, 0, 0, 64), (2, 64, 64, 32), (3, 64, 96, 32))
FAR += tuple((n, 96, 128 + 16 * (n - 4), 16) for n in (4, 5, 6, 7))
PLANE = 16


def tables():
    level_of = np.zeros(128, np.int64)
    pool = np.zeros((128, 128), np.float32)
    row = 0
    for level in range(1, 8):
        for i in range(128 >> level):
            pool[row, i << level : (i + 1) << level] = 1.0
            level_of[row] = level
            row += 1
    level_of[127] = 99
    pick = np.zeros((3, 128, 512), np.float32)
    pick_far = np.zeros((128, 512), np.float32)
    compact = np.zeros((2, 128, 512), np.float32)
    for i in range(PLANE):
        for half in range(2):
            at = 32 * i + 16 * half
            for x in range(3):
                for r in range(4):
                    pick[x, 8 * i + 4 * half + r, at + 4 * x + r] = 1.0
            for r in range(2):
                pick_far[8 * i + 2 * half + r, at + 8 + r] = 1.0
            pick_far[8 * i + 4 + half, at + 10] = 1.0
            pick_far[8 * i + 6, at + 11] = 1.0
            for kv in range(2):
                for r in range(2):
                    compact[kv, 4 * i + 2 * half + r, at + 4 * kv + r] = 1.0
                compact[kv, 64 + 2 * i + half, at + 4 * kv + 2] = 1.0
                compact[kv, 96 + i, at + 4 * kv + 3] = 1.0
    blocks = [pick[0], pick[1], pick[2], pick_far, compact[0], compact[1]]
    halves = np.concatenate(blocks, axis=0)
    places = np.concatenate([block.T for block in blocks], axis=1)
    small = np.zeros((192, 256), np.float32)
    small[0:128, :128] = pool
    small[0:128, 128:256] = pool.T
    for x in range(3):
        for r in range(4):
            small[128 + 4 * x + r, 64 * x + 16 * r : 64 * x + 16 * r + 16] = 1.0
        for r in range(2):
            small[144 + 4 * x + r, 64 * x + 32 * r : 64 * x + 32 * r + 32] = 1.0
        small[146 + 4 * x : 148 + 4 * x, 64 * x : 64 * x + 64] = 1.0
    for r in range(32):
        small[160 + r, r] = 1.0
        small[160 + r, 32 + r // 2] = 2.0**-0.5
    ancestor = np.where(pool.T > 0, 0.0, LOW)
    row_scale = np.where(level_of < 8, 2.0 ** (-level_of / 2.0), 0.0)[:, None] * np.ones((1, 128))
    half_scale = 2.0 ** (-np.array([4] * 16 + [5, 5, 6, 7] * 4) / 2.0)
    shard = np.arange(128) // 8
    across = np.where(shard[:, None] // 8 != shard[None, :] // 8, 0.0, LOW)
    near = np.full((48, 256), LOW)
    for r in range(48):
        for k in range(128):
            if level_of[64 + r] == (2 if k % 64 < 32 else 3):
                near[r, k] = 0.0
    far = np.full((128, 256), LOW)
    for r in range(128):
        for k in range(192):
            if level_of[120 + r % 8] == 5 + k // 64:
                far[r, k] = 0.0
    singles = np.concatenate(
        [
            np.concatenate([ancestor, row_scale], axis=1),
            np.concatenate([np.eye(128), across], axis=1),
            np.repeat(half_scale[:, None], 256, axis=1),
            near,
            far,
        ],
        axis=0,
    )
    return small, halves, places, singles.astype(np.float32)


T_POOL, T_HALF, T_GATHER = 0, 128, 160
P_PICK, P_FAR, P_COMPACT = 0, 384, 512
S_ANC, S_DIAG, S_HALF, S_NEAR, S_FAR = 0, 128, 256, 288, 336
S_ROWS = 464

C_ENTRY, C_EXIT, C_ONE, C_SHARE, C_PART, C_ONE_BACK = 0, 4, 8, 9, 10, 11
C_NEAR, C_NEAR_BACK, C_FAR, C_FAR_BACK = 11, 14, 17, 24
C_ROWS, C_SUMS, C_ADJ, C_DROWS, C_COARSE = 32, 64, 80, 96, 128
COPIES = 129


def mm(a, b):
    return lax.dot_general(a, b, (((1,), (0,)), ((), ())), preferred_element_type=F32)


def mm_nt(a, b):
    return lax.dot_general(a, b, (((1,), (1,)), ((), ())), preferred_element_type=F32)


def mm_tn(a, b):
    return lax.dot_general(a, b, (((0,), (0,)), ((), ())), preferred_element_type=F32)


def flipped(index, mask):
    for bit in range(8):
        if mask >> bit & 1:
            own = lax.rem(lax.div(index, 1 << bit), 2)
            index = index + (1 << bit) * (1 - 2 * own)
    return index


def kernel(
    heads,
    unroll,
    key_hbm, value_hbm, query_hbm, grad_hbm, small_hbm, half_hbm, place_hbm, single_hbm,
    att_hbm, dquery_hbm, dkey_hbm, dvalue_hbm, coarse_hbm, far_hbm,
    small_tab, half_tab, place_tab, single_tab, raw_in, rows_in, coarse_kv, coarse_q, one_kv, near_kv,
    rows_send, rows_recv, far_q, far_send, far_kv, pair_kv,
    local_scores, local_dprob, expo_one, expo_near, expo_far, numer, tops, totals,
    sums_send, sums_recv, adj_send, adj_recv, dfar_q, drows_send,
    dfar_send, dfar_recv,
    att_buf, dquery_buf, dkv_buf, local_ds, local_probs, adjoint, offset, dcoarse_q,
    part_grad, swap_grad, send_grad, recv_grad, one_part, one_recv, coarse_grad,
    load_sem, store_sem, self_sem, send_sem, recv_sem,
):
    seq = lax.axis_index("seq")
    head = lax.axis_index("head")
    width = heads * DH
    core = lax.rem(seq, 2)
    place = lax.rem(seq, PLANE)
    chip = lax.div(place, 2)
    mate = (seq, 1 - head)
    twin = (flipped(seq, 1), head)
    near_dev = {n: (flipped(seq, n << 1), head) for n, _, _, _ in NEAR}
    far_dev = {n: (flipped(seq, n << 4), head) for n, _, _, _ in FAR}
    peers = []
    for m in range(PLANE):
        there = flipped(seq, m)
        slot = lax.rem(there, PLANE)
        peers.append(((there, head), slot, lax.div(slot, 2), lax.rem(slot, 2)))
    mine = pl.ds(pl.multiple_of(head * width, width), width)
    theirs = pl.ds(pl.multiple_of((1 - head) * width, width), width)
    sources = (key_hbm, value_hbm, query_hbm, grad_hbm)

    def remote(src, dst, slot, device):
        return pltpu.make_async_remote_copy(
            src_ref=src, dst_ref=dst, send_sem=send_sem.at[slot], recv_sem=recv_sem.at[slot],
            device_id=device, device_id_type=MESH,
        )

    def slab(slot, rows):
        return pl.ds(pl.multiple_of(slot * rows, rows), rows)

    loads = [
        pltpu.make_async_copy(ref.at[:, mine], rows_in.at[i, pl.ds(0, 64)], load_sem.at[i])
        for i, ref in enumerate(sources)
    ]
    table_loads = [
        pltpu.make_async_copy(small_hbm, small_tab, load_sem.at[4]),
        pltpu.make_async_copy(single_hbm, single_tab, load_sem.at[5]),
        pltpu.make_async_copy(half_hbm, half_tab, load_sem.at[9]),
        pltpu.make_async_copy(place_hbm, place_tab, load_sem.at[10]),
    ]
    raw_loads = [
        pltpu.make_async_copy(ref, raw_in.at[pl.ds(64 * i, 64)], load_sem.at[6 + i]) for i, ref in enumerate(sources[:3])
    ]
    coarse_store = pltpu.make_async_copy(coarse_grad.at[0], coarse_hbm.at[:, mine], store_sem.at[4])
    coarse_exit = remote(coarse_grad.at[1], coarse_hbm.at[:, mine], C_COARSE, mate)
    coarse_wait = remote(coarse_grad.at[1], coarse_hbm.at[:, theirs], C_COARSE, mate)
    entry = [
        remote(ref.at[:, theirs], rows_in.at[i, pl.ds(64, 64)], C_ENTRY + i, mate)
        for i, ref in enumerate(sources)
    ]
    one_swap = remote(coarse_kv.at[:, pl.ds(0, 64)], one_kv, C_ONE, twin)
    near_copies = [
        remote(coarse_kv.at[:, pl.ds(src, count)], near_kv.at[0, :, pl.ds(dst, count)], C_NEAR + n, near_dev[n])
        for n, src, dst, count in NEAR
    ]
    share = remote(near_kv.at[0], near_kv.at[1], C_SHARE, twin)
    far_copies = [
        remote(far_send.at[pl.ds(src, count)], far_kv.at[pl.ds(dst, count)], C_FAR + n, far_dev[n])
        for n, src, dst, count in FAR
    ]
    far_back = [
        remote(dfar_send.at[pl.ds(dst, count)], dfar_recv.at[pl.ds(dst, count)], C_FAR_BACK + n, far_dev[n])
        for n, _, dst, count in FAR
    ]
    part_swap = remote(part_grad.at[1], swap_grad, C_PART, twin)
    near_back = [
        remote(send_grad.at[:, pl.ds(dst, count)], recv_grad.at[:, pl.ds(dst, count)], C_NEAR_BACK + n, near_dev[n])
        for n, _, dst, count in NEAR
    ]
    one_back = remote(one_part, one_recv, C_ONE_BACK, twin)

    class Spread:
        def __init__(self, which, base, send, recv, rows):
            self.local = pltpu.make_async_copy(
                send.at[chip, core], recv.at[slab(place, rows)], self_sem.at[which]
            )
            self.out = []
            self.come = []
            for m in range(1, PLANE):
                device, slot, owner, group = peers[m]
                self.out.append(remote(send.at[owner, group], recv.at[slab(place, rows)], base + m, device))
                self.come.append(remote(send.at[owner, group], recv.at[slab(slot, rows)], base + m, device))

        def start(self):
            for copy in self.out:
                copy.start()
            self.local.start()

        def wait_recv(self):
            self.local.wait()
            for copy in self.come:
                copy.wait_recv()

        def wait_send(self):
            for copy in self.out:
                copy.wait_send()

    class Return(Spread):
        def __init__(self, which, base, send, recv, rows):
            self.local = pltpu.make_async_copy(
                send.at[slab(place, rows)], recv.at[chip, core], self_sem.at[which]
            )
            self.out = []
            self.come = []
            for m in range(1, PLANE):
                device, slot, owner, group = peers[m]
                self.out.append(remote(send.at[slab(slot, rows)], recv.at[chip, core], base + m, device))
                self.come.append(remote(send.at[slab(slot, rows)], recv.at[owner, group], base + m, device))

    class Rows:
        def __init__(self, which, base, pairs):
            self.local = pltpu.make_async_copy(*pairs(0, 0)[:2], self_sem.at[which])
            self.out = []
            self.come = []
            for side in (0, 1):
                for m in range(PLANE):
                    if side == 0 and m == 0:
                        continue
                    src, dst, land = pairs(side, m)
                    device = (peers[m][0][0], mate[1] if side else head)
                    self.out.append(remote(src, dst, base + 16 * side + m, device))
                    self.come.append(remote(src, land, base + 16 * side + m, device))

        start = Spread.start
        wait_recv = Spread.wait_recv
        wait_send = Spread.wait_send

    def message_pairs(side, m):
        _, slot, owner, group = peers[m]
        group_of_heads = mate[1] if side else head
        return (
            rows_send.at[group_of_heads * heads + owner, group],
            rows_recv.at[slab(2 * place + side, 16)],
            rows_recv.at[slab(2 * slot + side, 16)],
        )

    def drow_pairs(side, m):
        _, slot, owner, group = peers[m]
        group_of_heads = mate[1] if side else head
        return (
            drows_send.at[slab(2 * slot + side, 16)],
            far_hbm.at[slab(2 * (head * heads + chip) + core, 16)],
            far_hbm.at[slab(2 * (group_of_heads * heads + owner) + group, 16)],
        )

    rows_out = Rows(0, C_ROWS, message_pairs)
    sums_back = Return(1, C_SUMS, sums_send, sums_recv, 16)
    adj_out = Spread(2, C_ADJ, adj_send, adj_recv, 16)
    drows_back = Rows(3, C_DROWS, drow_pairs)

    results = ((att_buf, att_hbm), (dquery_buf, dquery_hbm), (dkv_buf.at[0], dkey_hbm), (dkv_buf.at[1], dvalue_hbm))
    stores = [
        pltpu.make_async_copy(buf.at[pl.ds(0, 64)], out.at[:, mine], store_sem.at[i])
        for i, (buf, out) in enumerate(results)
    ]
    exits = [
        remote(buf.at[pl.ds(64, 64)], out.at[:, mine], C_EXIT + i, mate)
        for i, (buf, out) in enumerate(results)
    ]
    exit_waits = [
        remote(buf.at[pl.ds(64, 64)], out.at[:, theirs], C_EXIT + i, mate)
        for i, (buf, out) in enumerate(results)
    ]

    for copy in raw_loads + table_loads + loads:
        copy.start()
    barrier = pltpu.get_barrier_semaphore()
    partners = [peer[0] for peer in peers[1:]] + [(peer[0][0], mate[1]) for peer in peers] + list(far_dev.values())
    for device in partners:
        pl.semaphore_signal(barrier, inc=1, device_id=device, device_id_type=MESH)
    def columns(h):
        return pl.ds(pl.multiple_of(h * DH, DH), DH)

    def each_head(*steps, count=heads):
        def body(i, carry):
            for step in steps:
                for j in range(unroll):
                    step(i * unroll + j)
            return carry

        lax.fori_loop(0, count // unroll, body, 0)

    for copy in table_loads[:2]:
        copy.wait()
    everything = pl.ds(0, 128)
    right = pl.ds(128, 128)

    for copy in raw_loads:
        copy.wait()

    def pool_half(h):
        rows = mm(small_tab[pl.ds(T_HALF, 32), pl.ds(0, 192)], raw_in[:, columns(h)])
        rows = (rows * single_tab[pl.ds(S_HALF, 32), everything]).astype(BF16)
        rows_send[h, 0] = rows[0:16]
        rows_send[h, 1] = rows[16:32]

    each_head(pool_half, count=2 * heads)
    pl.semaphore_wait(barrier, len(partners))
    rows_out.start()
    for copy in entry:
        copy.start()

    def pooled(which, h):
        rows = mm(small_tab[pl.ds(T_POOL, 112), pl.ds(0, 128)], rows_in[which, :, columns(h)])
        return (rows * single_tab[pl.ds(S_ANC, 112), right]).astype(BF16)

    for copy in table_loads[2:]:
        copy.wait()
    rows_out.wait_recv()

    def picked(row, count):
        return mm(half_tab[pl.ds(row, count)], rows_recv[...]).astype(BF16)

    @pl.when(core == 1)
    def _():
        for kv in (0, 1):
            far_send[:, pl.ds(128 * kv, 128)] = picked(P_COMPACT + 128 * kv, 112)
        for copy in far_copies:
            copy.start()
        far_q[...] = picked(P_FAR, 128)

    @pl.when(core == 0)
    def _():
        for kv in (0, 1):
            pair_kv[:, pl.ds(128 * kv, 128)] = picked(P_PICK + 128 * kv, 128)
        far_q[...] = picked(P_PICK + 256, 128)

    for kv in (0, 1):
        loads[kv].wait()
        entry[kv].wait_recv()

    def pool_rows(h):
        cols = columns(h)
        coarse_kv[0, :, cols] = pooled(0, h)
        coarse_kv[1, :, cols] = pooled(1, h)

    each_head(pool_rows)
    for copy in near_copies:
        copy.start()
    one_swap.start()

    loads[2].wait()
    entry[2].wait_recv()

    def pool_queries(h):
        coarse_q[:, columns(h)] = pooled(2, h)

    each_head(pool_queries)

    def to_row(column, start):
        count = column.shape[0]
        picked = column * single_tab[pl.ds(S_DIAG + start, count), everything]
        return jnp.sum(picked, axis=0, keepdims=True)

    def attend(queries, keys, vals, mask):
        scores = mm_nt(queries, keys) * SCALE
        if mask is not None:
            scores = scores + mask
        top = jnp.maximum(jnp.max(scores, axis=1, keepdims=True), FLOOR)
        weights = jnp.exp(scores - top)
        total = jnp.sum(weights, axis=1, keepdims=True)
        return weights, top, total, mm(weights.astype(BF16), vals)

    def attend_back(weights, adj, shift, queries, keys, vals):
        inner = mm_nt(adj, vals) - shift
        dscore = (weights * inner).astype(BF16)
        dkeys = mm_tn(dscore, queries) * SCALE
        return mm(dscore, keys), dkeys, mm_tn(weights.astype(BF16), adj)

    def near_rows(kv, h):
        return jnp.concatenate([near_kv[0, kv, :, columns(h)], near_kv[1, kv, :, columns(h)]], axis=0)

    def forward_one(h):
        cols = columns(h)
        weights, top, total, sums = attend(
            coarse_q[pl.ds(0, 64), cols], one_kv[0, :, cols], one_kv[1, :, cols], None
        )
        expo_one[h] = weights
        numer[h, pl.ds(0, 64)] = sums
        tops[h, pl.ds(0, 1)] = to_row(top, 0)
        totals[h, pl.ds(0, 1)] = to_row(total, 0)

    def forward_near(h):
        weights, top, total, sums = attend(
            coarse_q[pl.ds(64, 48), columns(h)], near_rows(0, h), near_rows(1, h),
            single_tab[pl.ds(S_NEAR, 48), everything],
        )
        expo_near[h] = weights
        numer[h, pl.ds(64, 48)] = sums
        tops[h, pl.ds(1, 1)] = to_row(top, 64)
        totals[h, pl.ds(1, 1)] = to_row(total, 64)

    def forward_far(keys, vals, mask, span):
        weights, top, total, sums = attend(far_q[...], keys, vals, mask)
        expo_far[:, pl.ds(0, span)] = weights
        lanes = lax.broadcasted_iota(jnp.int32, (128, 128), 1)
        pair = jnp.where(lanes < 64, top, total)
        whole = jnp.concatenate([sums.reshape(PLANE, 8, 128), pair.reshape(PLANE, 8, 128)], axis=1)
        sums_send[...] = whole.reshape(PLANE * 16, 128)

    @pl.when(core == 0)
    def _():
        forward_far(
            pair_kv[:, everything], pair_kv[:, right], single_tab[pl.ds(S_DIAG, 128), right], 128
        )

    @pl.when(core == 1)
    def _():
        for copy in far_copies:
            copy.wait_recv()
        forward_far(
            far_kv[:, everything], far_kv[:, right], single_tab[pl.ds(S_FAR, 128), pl.ds(0, 192)], 192
        )

    sums_back.start()

    one_swap.wait_recv()
    each_head(forward_one)
    for copy in near_copies:
        copy.wait_recv()
    share.start()

    loads[3].wait()
    entry[3].wait_recv()

    def score_local(h):
        cols = columns(h)
        local_scores[h] = mm_nt(rows_in[2, :, cols], rows_in[0, :, cols]) * SCALE
        local_dprob[h] = mm_nt(rows_in[3, :, cols], rows_in[1, :, cols])

    each_head(score_local)
    share.wait_recv()
    each_head(forward_near)
    sums_back.wait_recv()

    def combine(h):
        cols = columns(h)
        top_row = tops[h, pl.ds(0, 1)] + tops[h, pl.ds(1, 1)]
        total_row = totals[h, pl.ds(0, 1)] + totals[h, pl.ds(1, 1)]
        for group in (0, 1):
            top_row = top_row + to_row(sums_recv[h, group, pl.ds(8, 8), pl.ds(0, 1)], 112 + 8 * group)
            total_row = total_row + to_row(sums_recv[h, group, pl.ds(8, 8), pl.ds(64, 1)], 112 + 8 * group)
        scores = local_scores[h]
        coarse = single_tab[pl.ds(S_ANC, 128), everything] + top_row
        top = jnp.max(jnp.maximum(scores, coarse), axis=1, keepdims=True)
        expo = jnp.exp(scores - top)
        factor = jnp.exp(coarse - top)
        total = jnp.sum(expo + factor * total_row, axis=1, keepdims=True)
        inverse = 1.0 / total
        numer_all = jnp.concatenate(
            [numer[h], sums_recv[h, 0, pl.ds(0, 8)], sums_recv[h, 1, pl.ds(0, 8)]], axis=0
        ).astype(BF16)
        outcome = (mm(expo.astype(BF16), rows_in[1, :, cols]) + mm(factor.astype(BF16), numer_all)) * inverse
        att_buf[:, cols] = outcome.astype(BF16)
        grad = rows_in[3, :, cols]
        dots = jnp.sum(grad.astype(F32) * outcome, axis=1, keepdims=True)
        probs = expo * inverse
        weight = (factor * inverse).astype(BF16)
        local_probs[h] = probs.astype(BF16)
        local_ds[h] = (probs * (local_dprob[h] - dots)).astype(BF16)
        adj = mm_tn(weight, grad)
        adjoint[h] = adj.astype(BF16)
        dots_wide = jnp.broadcast_to(dots, (128, 128))
        dots_high = dots_wide.astype(BF16)
        dots_low = (dots_wide - dots_high.astype(F32)).astype(BF16)
        shift = mm_tn(weight, dots_high) + mm_tn(weight, dots_low)
        offset[h] = shift
        for group in (0, 1):
            low = 112 + 8 * group
            adj_send[h, group, pl.ds(0, 8)] = adj[low : low + 8]
            adj_send[h, group, pl.ds(8, 8)] = shift[low : low + 8]

    each_head(combine)
    adj_out.start()
    stores[0].start()
    exits[0].start()

    def backward_near(h):
        cols = columns(h)
        dqueries, dkeys, dvals = attend_back(
            expo_near[h], adjoint[h, pl.ds(64, 48)], offset[h, pl.ds(64, 48), pl.ds(0, 1)],
            coarse_q[pl.ds(64, 48), cols], near_rows(0, h), near_rows(1, h),
        )
        dcoarse_q[h, pl.ds(64, 48)] = dqueries
        for side in (0, 1):
            part_grad[side, 0, :, cols] = dkeys[64 * side : 64 * side + 64].astype(BF16)
            part_grad[side, 1, :, cols] = dvals[64 * side : 64 * side + 64].astype(BF16)

    def backward_one(h):
        cols = columns(h)
        dqueries, dkeys, dvals = attend_back(
            expo_one[h], adjoint[h, pl.ds(0, 64)], offset[h, pl.ds(0, 64), pl.ds(0, 1)],
            coarse_q[pl.ds(0, 64), cols], one_kv[0, :, cols], one_kv[1, :, cols],
        )
        dcoarse_q[h, pl.ds(0, 64)] = dqueries
        one_part[0, :, cols] = dkeys.astype(BF16)
        one_part[1, :, cols] = dvals.astype(BF16)

    each_head(backward_near)
    part_swap.start()
    each_head(backward_one)
    one_back.start()

    def unpooled(rows):
        count = rows.shape[0]
        scaled = rows * single_tab[pl.ds(S_ANC, count), right]
        return mm(small_tab[pl.ds(T_POOL, 128), pl.ds(128, count)], scaled.astype(BF16))

    def query_total(h):
        cols = columns(h)
        total = mm(local_ds[h], rows_in[0, :, cols]) + unpooled(dcoarse_q[h])
        dquery_buf[:, cols] = (total * SCALE).astype(BF16)

    each_head(query_total)
    stores[1].start()
    exits[1].start()
    part_swap.wait_recv()

    def sum_near(h):
        cols = columns(h)
        for kv in (0, 1):
            both = part_grad[0, kv, :, cols].astype(F32) + swap_grad[kv, :, cols].astype(F32)
            send_grad[kv, :, cols] = both.astype(BF16)

    each_head(sum_near)
    for copy in near_back:
        copy.start()
    one_back.wait_recv()

    def local_back(h):
        cols = columns(h)
        dkeys = mm_tn(local_ds[h], rows_in[2, :, cols]) * SCALE
        dvals = mm_tn(local_probs[h], rows_in[3, :, cols])
        for kv, total in ((0, dkeys), (1, dvals)):
            total = total + unpooled(one_recv[kv, :, cols].astype(F32))
            dkv_buf[kv, :, cols] = total.astype(BF16)

    each_head(local_back)
    for i in (2, 3):
        stores[i].start()
        exits[i].start()

    adj_out.wait_recv()

    def backward_far(keys, vals, span):
        arrived = adj_recv[...].reshape(PLANE, 16, 128)
        adj = arrived[:, 0:8].reshape(128, 128).astype(BF16)
        shift = arrived[:, 8:16].reshape(128, 128)[:, 0:1]
        dqueries, dkeys, dvals = attend_back(expo_far[:, pl.ds(0, span)], adj, shift, far_q[...], keys, vals)
        return (dqueries * SCALE).astype(BF16), dkeys.astype(BF16), dvals.astype(BF16)

    @pl.when(core == 0)
    def _():
        dqueries, dkeys, dvals = backward_far(pair_kv[:, everything], pair_kv[:, right], 128)
        rows = jnp.concatenate([dkeys, dvals, dqueries], axis=0)
        drows_send[...] = mm(place_tab[:, pl.ds(P_PICK, 384)], rows).astype(BF16)

    @pl.when(core == 1)
    def _():
        dqueries, dkeys, dvals = backward_far(far_kv[:, everything], far_kv[:, right], 192)
        dfar_send[:, everything] = dkeys
        dfar_send[:, right] = dvals
        for copy in far_back:
            copy.start()
        dfar_q[...] = dqueries
        for copy in far_back:
            copy.wait_recv()
        came = dfar_recv[...].astype(F32)
        level_six = came[64:96] + came[96:128]
        level_seven = (came[128:144] + came[144:160]) + (came[160:176] + came[176:192])
        rows = jnp.concatenate([came[0:64], level_six, level_seven, jnp.zeros((16, 256), F32)], axis=0).astype(BF16)
        rows = jnp.concatenate([dfar_q[...], rows[:, 0:128], rows[:, 128:256]], axis=0)
        drows_send[...] = mm(place_tab[:, pl.ds(P_FAR, 384)], rows).astype(BF16)

    drows_back.start()

    for copy in near_back:
        copy.wait_recv()

    def gather_coarse(h):
        cols = columns(h)
        for kv in (0, 1):
            coarse = jnp.concatenate(
                [
                    recv_grad[kv, pl.ds(0, 32), cols].astype(F32),
                    recv_grad[kv, pl.ds(32, 16), cols].astype(F32)
                    + recv_grad[kv, pl.ds(48, 16), cols].astype(F32),
                ],
                axis=0,
            )
            total = mm(small_tab[pl.ds(T_GATHER, 32), pl.ds(0, 48)], coarse.astype(BF16)).astype(BF16)
            coarse_grad[0, pl.ds(16 * kv, 16), cols] = total[0:16]
            coarse_grad[1, pl.ds(16 * kv, 16), cols] = total[16:32]

    each_head(gather_coarse)
    coarse_store.start()
    coarse_exit.start()
    drows_back.wait_recv()

    for copy in entry + near_copies + near_back + [one_swap, share, part_swap, one_back, coarse_exit] + exits:
        copy.wait_send()
    for copy in (rows_out, sums_back, adj_out, drows_back):
        copy.wait_send()

    @pl.when(core == 1)
    def _():
        for copy in far_copies + far_back:
            copy.wait_send()

    for copy in stores + [coarse_store]:
        copy.wait()
    for copy in exit_waits + [coarse_wait]:
        copy.wait_recv()


def last_kernel(
    heads, att_ref, dquery_ref, dkey_ref, dvalue_ref, coarse_ref, far_ref, att_out, dquery_out, dkey_out, dvalue_out
):
    att_out[...] = att_ref[...]
    rows = lax.broadcasted_iota(jnp.int32, (64, 32), 0)
    parents = lax.broadcasted_iota(jnp.int32, (64, 32), 1)

    def among(first, count, span):
        at = parents - first
        return (at >= 0) & (at < count) & (rows >= span * at) & (rows < span * at + span)

    spread = jnp.where(among(0, 16, 4), 0.5, 0.0).astype(BF16)[:, 0:16]
    far = [
        jnp.where(among(4 * x, 4, 16), 0.25, 0.0)
        + jnp.where(among(16 + 4 * x, 2, 32), 2.0**-2.5, 0.0)
        + jnp.where(among(18 + 4 * x, 1, 64), 2.0**-3, 0.0)
        + jnp.where(among(19 + 4 * x, 1, 64), 2.0**-3.5, 0.0)
        for x in range(3)
    ]
    far = jnp.concatenate(far, axis=0).astype(BF16)
    for h in range(heads):
        cols = pl.ds(DH * h, DH)
        added = mm(far, far_ref[pl.ds(32 * h, 32)])
        near = [mm(spread, coarse_ref[pl.ds(16 * kv, 16), cols]) for kv in (0, 1)]
        dkey_out[:, cols] = (dkey_ref[:, cols].astype(F32) + added[0:64] + near[0]).astype(BF16)
        dvalue_out[:, cols] = (dvalue_ref[:, cols].astype(F32) + added[64:128] + near[1]).astype(BF16)
        dquery_out[:, cols] = (dquery_ref[:, cols].astype(F32) + added[128:192]).astype(BF16)


def solution(mesh):
    small, halves, places, singles = tables()
    small, halves, places = (table.astype(BF16) for table in (small, halves, places))
    unroll = 4

    def local(queries, key_rows, values, out_grad):
        rows, columns = queries.shape
        width = columns // 2
        heads = width // DH
        tall = 2 * rows
        anywhere = pl.BlockSpec(memory_space=pl.ANY)
        out = jax.ShapeDtypeStruct((rows, columns), BF16)
        vmem = pltpu.VMEM
        scratch = [
            vmem((192, 256), BF16),
            vmem((768, 512), BF16),
            vmem((512, 768), BF16),
            vmem((S_ROWS, 256), F32),
            vmem((3 * rows, columns), BF16),
            vmem((4, tall, width), BF16),
            vmem((2, 112, width), BF16),
            vmem((112, width), BF16),
            vmem((2, 64, width), BF16),
            vmem((2, 2, 64, width), BF16),
            vmem((2 * heads, 2, 16, 128), BF16),
            vmem((PLANE * 32, 128), BF16),
            vmem((128, 128), BF16),
            vmem((112, 256), BF16),
            vmem((192, 256), BF16),
            vmem((128, 256), BF16),
            vmem((heads, 128, 128), F32),
            vmem((heads, 128, 128), F32),
            vmem((heads, 64, 64), F32),
            vmem((heads, 48, 128), F32),
            vmem((128, 192), F32),
            vmem((heads, 112, 128), F32),
            vmem((heads, 8, 128), F32),
            vmem((heads, 8, 128), F32),
            vmem((PLANE * 16, 128), F32),
            vmem((heads, 2, 16, 128), F32),
            vmem((heads, 2, 16, 128), F32),
            vmem((PLANE * 16, 128), F32),
            vmem((128, 128), BF16),
            vmem((PLANE * 32, 128), BF16),
            vmem((192, 256), BF16),
            vmem((192, 256), BF16),
            vmem((tall, width), BF16),
            vmem((tall, width), BF16),
            vmem((2, tall, width), BF16),
            vmem((heads, 128, 128), BF16),
            vmem((heads, 128, 128), BF16),
            vmem((heads, 128, 128), BF16),
            vmem((heads, 128, 128), F32),
            vmem((heads, 112, 128), F32),
            vmem((2, 2, 64, width), BF16),
            vmem((2, 64, width), BF16),
            vmem((2, 64, width), BF16),
            vmem((2, 64, width), BF16),
            vmem((2, 64, width), BF16),
            vmem((2, 64, width), BF16),
            vmem((2, 32, width), BF16),
            pltpu.SemaphoreType.DMA((11,)),
            pltpu.SemaphoreType.DMA((5,)),
            pltpu.SemaphoreType.DMA((4,)),
            pltpu.SemaphoreType.DMA((COPIES,)),
            pltpu.SemaphoreType.DMA((COPIES,)),
        ]
        parts = pl.pallas_call(
            functools.partial(kernel, heads, unroll),
            out_shape=(out,) * 4
            + (jax.ShapeDtypeStruct((32, columns), BF16), jax.ShapeDtypeStruct((64 * heads, 128), BF16)),
            in_specs=[anywhere] * 8,
            out_specs=(anywhere,) * 6,
            scratch_shapes=scratch,
            compiler_params=pltpu.CompilerParams(
                collective_id=0, has_side_effects=True, vmem_limit_bytes=60 << 20
            ),
            name="sibling_attention",
        )(key_rows, values, queries, out_grad, *(jnp.asarray(table) for table in (small, halves, places, singles)))
        whole = pl.BlockSpec(memory_space=pltpu.VMEM)
        return pl.pallas_call(
            functools.partial(last_kernel, 2 * heads),
            out_shape=(out,) * 4,
            in_specs=[whole] * 6,
            out_specs=(whole,) * 4,
            name="coarse_rows_added",
        )(*parts)

    spec = P(("seq", "head"), None)
    return jax.shard_map(
        local, mesh=mesh, in_specs=(spec,) * 4, out_specs=(spec,) * 4, check_vma=False
    )
```

```python
import functools
import math

import jax
import jax.numpy as jnp
import numpy as np
from jax import lax
from jax.experimental import pallas as pl
from jax.experimental.pallas import tpu as pltpu
from jax.sharding import PartitionSpec as P

MESH = pl.DeviceIdType.MESH
BF16 = jnp.bfloat16
F32 = jnp.float32
DH = 128
SCALE = 1.0 / math.sqrt(DH)
LOW = -1e30
FLOOR = -1e29

NEAR = ((1, 64, 0, 32), (2, 96, 32, 16), (3, 96, 48, 16))
FAR = ((1, 0, 0, 64), (2, 64, 64, 32), (3, 64, 96, 32))
FAR += tuple((n, 96, 128 + 16 * (n - 4), 16) for n in (4, 5, 6, 7))
PLANE = 16


def tables():
    level_of = np.zeros(128, np.int64)
    pool = np.zeros((128, 128), np.float32)
    row = 0
    for level in range(1, 8):
        for i in range(128 >> level):
            pool[row, i << level : (i + 1) << level] = 1.0
            level_of[row] = level
            row += 1
    level_of[127] = 99
    pick = np.zeros((3, 128, 512), np.float32)
    pick_far = np.zeros((128, 512), np.float32)
    compact = np.zeros((2, 128, 512), np.float32)
    for i in range(PLANE):
        for half in range(2):
            at = 32 * i + 16 * half
            for x in range(3):
                for r in range(4):
                    pick[x, 8 * i + 4 * half + r, at + 4 * x + r] = 1.0
            for r in range(2):
                pick_far[8 * i + 2 * half + r, at + 8 + r] = 1.0
            pick_far[8 * i + 4 + half, at + 10] = 1.0
            pick_far[8 * i + 6, at + 11] = 1.0
            for kv in range(2):
                for r in range(2):
                    compact[kv, 4 * i + 2 * half + r, at + 4 * kv + r] = 1.0
                compact[kv, 64 + 2 * i + half, at + 4 * kv + 2] = 1.0
                compact[kv, 96 + i, at + 4 * kv + 3] = 1.0
    blocks = [pick[0], pick[1], pick[2], pick_far, compact[0], compact[1]]
    halves = np.concatenate(blocks, axis=0)
    places = np.concatenate([block.T for block in blocks], axis=1)
    small = np.zeros((192, 256), np.float32)
    small[0:128, :128] = pool
    small[0:128, 128:256] = pool.T
    for x in range(3):
        for r in range(4):
            small[128 + 4 * x + r, 64 * x + 16 * r : 64 * x + 16 * r + 16] = 1.0
        for r in range(2):
            small[144 + 4 * x + r, 64 * x + 32 * r : 64 * x + 32 * r + 32] = 1.0
        small[146 + 4 * x : 148 + 4 * x, 64 * x : 64 * x + 64] = 1.0
    for r in range(32):
        small[160 + r, r] = 1.0
        small[160 + r, 32 + r // 2] = 2.0**-0.5
    ancestor = np.where(pool.T > 0, 0.0, LOW)
    row_scale = np.where(level_of < 8, 2.0 ** (-level_of / 2.0), 0.0)[:, None] * np.ones((1, 128))
    half_scale = 2.0 ** (-np.array([4] * 16 + [5, 5, 6, 7] * 4) / 2.0)
    shard = np.arange(128) // 8
    across = np.where(shard[:, None] // 8 != shard[None, :] // 8, 0.0, LOW)
    near = np.full((48, 256), LOW)
    for r in range(48):
        for k in range(128):
            if level_of[64 + r] == (2 if k % 64 < 32 else 3):
                near[r, k] = 0.0
    far = np.full((128, 256), LOW)
    for r in range(128):
        for k in range(192):
            if level_of[120 + r % 8] == 5 + k // 64:
                far[r, k] = 0.0
    singles = np.concatenate(
        [
            np.concatenate([ancestor, row_scale], axis=1),
            np.concatenate([np.eye(128), across], axis=1),
            np.repeat(half_scale[:, None], 256, axis=1),
            near,
            far,
        ],
        axis=0,
    )
    return small, halves, places, singles.astype(np.float32)


T_POOL, T_HALF, T_GATHER = 0, 128, 160
P_PICK, P_FAR, P_COMPACT = 0, 384, 512
S_ANC, S_DIAG, S_HALF, S_NEAR, S_FAR = 0, 128, 256, 288, 336
S_ROWS = 464

C_ENTRY, C_EXIT, C_ONE, C_SHARE, C_PART, C_ONE_BACK = 0, 4, 8, 9, 10, 11
C_NEAR, C_NEAR_BACK, C_FAR, C_FAR_BACK = 11, 14, 17, 24
C_ROWS, C_SUMS, C_ADJ, C_DROWS, C_COARSE = 32, 64, 80, 96, 128
COPIES = 129


def mm(a, b):
    return lax.dot_general(a, b, (((1,), (0,)), ((), ())), preferred_element_type=F32)


def mm_nt(a, b):
    return lax.dot_general(a, b, (((1,), (1,)), ((), ())), preferred_element_type=F32)


def mm_tn(a, b):
    return lax.dot_general(a, b, (((0,), (0,)), ((), ())), preferred_element_type=F32)


def flipped(index, mask):
    for bit in range(8):
        if mask >> bit & 1:
            own = lax.rem(lax.div(index, 1 << bit), 2)
            index = index + (1 << bit) * (1 - 2 * own)
    return index


def kernel(
    heads,
    key_hbm, value_hbm, query_hbm, grad_hbm, small_hbm, half_hbm, place_hbm, single_hbm,
    att_hbm, dquery_hbm, dkey_hbm, dvalue_hbm, coarse_hbm, far_hbm,
    small_tab, half_tab, place_tab, single_tab, raw_in, rows_in, coarse_kv, coarse_q, one_kv, near_kv,
    rows_send, rows_recv, far_q, far_send, far_kv, pair_kv,
    local_scores, local_dprob, expo_one, expo_near, expo_far, numer, tops, totals,
    sums_send, sums_recv, adj_send, adj_recv, dfar_q, drows_send,
    dfar_send, dfar_recv,
    att_buf, dquery_buf, dkv_buf, local_ds, local_probs, adjoint, offset, dcoarse_q,
    part_grad, swap_grad, send_grad, recv_grad, one_part, one_recv, coarse_grad,
    load_sem, store_sem, self_sem, send_sem, recv_sem,
):
    seq = lax.axis_index("seq")
    head = lax.axis_index("head")
    width = heads * DH
    core = lax.rem(seq, 2)
    place = lax.rem(seq, PLANE)
    chip = lax.div(place, 2)
    mate = (seq, 1 - head)
    twin = (flipped(seq, 1), head)
    near_dev = {n: (flipped(seq, n << 1), head) for n, _, _, _ in NEAR}
    far_dev = {n: (flipped(seq, n << 4), head) for n, _, _, _ in FAR}
    peers = []
    for m in range(PLANE):
        there = flipped(seq, m)
        slot = lax.rem(there, PLANE)
        peers.append(((there, head), slot, lax.div(slot, 2), lax.rem(slot, 2)))
    mine = pl.ds(pl.multiple_of(head * width, width), width)
    theirs = pl.ds(pl.multiple_of((1 - head) * width, width), width)
    sources = (key_hbm, value_hbm, query_hbm, grad_hbm)

    def remote(src, dst, slot, device):
        return pltpu.make_async_remote_copy(
            src_ref=src, dst_ref=dst, send_sem=send_sem.at[slot], recv_sem=recv_sem.at[slot],
            device_id=device, device_id_type=MESH,
        )

    def slab(slot, rows):
        return pl.ds(pl.multiple_of(slot * rows, rows), rows)

    loads = [
        pltpu.make_async_copy(ref.at[:, mine], rows_in.at[i, pl.ds(0, 64)], load_sem.at[i])
        for i, ref in enumerate(sources)
    ]
    table_loads = [
        pltpu.make_async_copy(small_hbm, small_tab, load_sem.at[4]),
        pltpu.make_async_copy(single_hbm, single_tab, load_sem.at[5]),
        pltpu.make_async_copy(half_hbm, half_tab, load_sem.at[9]),
        pltpu.make_async_copy(place_hbm, place_tab, load_sem.at[10]),
    ]
    raw_loads = [
        pltpu.make_async_copy(ref, raw_in.at[pl.ds(64 * i, 64)], load_sem.at[6 + i]) for i, ref in enumerate(sources[:3])
    ]
    coarse_store = pltpu.make_async_copy(coarse_grad.at[0], coarse_hbm.at[:, mine], store_sem.at[4])
    coarse_exit = remote(coarse_grad.at[1], coarse_hbm.at[:, mine], C_COARSE, mate)
    coarse_wait = remote(coarse_grad.at[1], coarse_hbm.at[:, theirs], C_COARSE, mate)
    entry = [
        remote(ref.at[:, theirs], rows_in.at[i, pl.ds(64, 64)], C_ENTRY + i, mate)
        for i, ref in enumerate(sources)
    ]
    one_swap = remote(coarse_kv.at[:, pl.ds(0, 64)], one_kv, C_ONE, twin)
    near_copies = [
        remote(coarse_kv.at[:, pl.ds(src, count)], near_kv.at[0, :, pl.ds(dst, count)], C_NEAR + n, near_dev[n])
        for n, src, dst, count in NEAR
    ]
    share = remote(near_kv.at[0], near_kv.at[1], C_SHARE, twin)
    far_copies = [
        remote(far_send.at[pl.ds(src, count)], far_kv.at[pl.ds(dst, count)], C_FAR + n, far_dev[n])
        for n, src, dst, count in FAR
    ]
    far_back = [
        remote(dfar_send.at[pl.ds(dst, count)], dfar_recv.at[pl.ds(dst, count)], C_FAR_BACK + n, far_dev[n])
        for n, _, dst, count in FAR
    ]
    part_swap = remote(part_grad.at[1], swap_grad, C_PART, twin)
    near_back = [
        remote(send_grad.at[:, pl.ds(dst, count)], recv_grad.at[:, pl.ds(dst, count)], C_NEAR_BACK + n, near_dev[n])
        for n, _, dst, count in NEAR
    ]
    one_back = remote(one_part, one_recv, C_ONE_BACK, twin)

    class Spread:
        def __init__(self, which, base, send, recv, rows):
            self.local = pltpu.make_async_copy(
                send.at[chip, core], recv.at[slab(place, rows)], self_sem.at[which]
            )
            self.out = []
            self.come = []
            for m in range(1, PLANE):
                device, slot, owner, group = peers[m]
                self.out.append(remote(send.at[owner, group], recv.at[slab(place, rows)], base + m, device))
                self.come.append(remote(send.at[owner, group], recv.at[slab(slot, rows)], base + m, device))

        def start(self):
            for copy in self.out:
                copy.start()
            self.local.start()

        def wait_recv(self):
            self.local.wait()
            for copy in self.come:
                copy.wait_recv()

        def wait_send(self):
            for copy in self.out:
                copy.wait_send()

    class Return(Spread):
        def __init__(self, which, base, send, recv, rows):
            self.local = pltpu.make_async_copy(
                send.at[slab(place, rows)], recv.at[chip, core], self_sem.at[which]
            )
            self.out = []
            self.come = []
            for m in range(1, PLANE):
                device, slot, owner, group = peers[m]
                self.out.append(remote(send.at[slab(slot, rows)], recv.at[chip, core], base + m, device))
                self.come.append(remote(send.at[slab(slot, rows)], recv.at[owner, group], base + m, device))

    class Rows:
        def __init__(self, which, base, pairs):
            self.local = pltpu.make_async_copy(*pairs(0, 0)[:2], self_sem.at[which])
            self.out = []
            self.come = []
            for side in (0, 1):
                for m in range(PLANE):
                    if side == 0 and m == 0:
                        continue
                    src, dst, land = pairs(side, m)
                    device = (peers[m][0][0], mate[1] if side else head)
                    self.out.append(remote(src, dst, base + 16 * side + m, device))
                    self.come.append(remote(src, land, base + 16 * side + m, device))

        start = Spread.start
        wait_recv = Spread.wait_recv
        wait_send = Spread.wait_send

    def message_pairs(side, m):
        _, slot, owner, group = peers[m]
        group_of_heads = mate[1] if side else head
        return (
            rows_send.at[group_of_heads * heads + owner, group],
            rows_recv.at[slab(2 * place + side, 16)],
            rows_recv.at[slab(2 * slot + side, 16)],
        )

    def drow_pairs(side, m):
        _, slot, owner, group = peers[m]
        group_of_heads = mate[1] if side else head
        return (
            drows_send.at[slab(2 * slot + side, 16)],
            far_hbm.at[slab(2 * (head * heads + chip) + core, 16)],
            far_hbm.at[slab(2 * (group_of_heads * heads + owner) + group, 16)],
        )

    rows_out = Rows(0, C_ROWS, message_pairs)
    sums_back = Return(1, C_SUMS, sums_send, sums_recv, 16)
    adj_out = Spread(2, C_ADJ, adj_send, adj_recv, 16)
    drows_back = Rows(3, C_DROWS, drow_pairs)

    results = ((att_buf, att_hbm), (dquery_buf, dquery_hbm), (dkv_buf.at[0], dkey_hbm), (dkv_buf.at[1], dvalue_hbm))
    stores = [
        pltpu.make_async_copy(buf.at[pl.ds(0, 64)], out.at[:, mine], store_sem.at[i])
        for i, (buf, out) in enumerate(results)
    ]
    exits = [
        remote(buf.at[pl.ds(64, 64)], out.at[:, mine], C_EXIT + i, mate)
        for i, (buf, out) in enumerate(results)
    ]
    exit_waits = [
        remote(buf.at[pl.ds(64, 64)], out.at[:, theirs], C_EXIT + i, mate)
        for i, (buf, out) in enumerate(results)
    ]

    for copy in raw_loads + table_loads + loads:
        copy.start()
    barrier = pltpu.get_barrier_semaphore()
    partners = [peer[0] for peer in peers[1:]] + [(peer[0][0], mate[1]) for peer in peers] + list(far_dev.values())
    for device in partners:
        pl.semaphore_signal(barrier, inc=1, device_id=device, device_id_type=MESH)
    def columns(h):
        return pl.ds(h * DH, DH)

    def each_head(*steps, count=heads):
        for step in steps:
            for h in range(count):
                step(h)

    for copy in table_loads[:2]:
        copy.wait()
    everything = pl.ds(0, 128)
    right = pl.ds(128, 128)

    for copy in raw_loads:
        copy.wait()

    def pool_half(h):
        rows = mm(small_tab[pl.ds(T_HALF, 32), pl.ds(0, 192)], raw_in[:, columns(h)])
        rows = (rows * single_tab[pl.ds(S_HALF, 32), everything]).astype(BF16)
        rows_send[h, 0] = rows[0:16]
        rows_send[h, 1] = rows[16:32]

    each_head(pool_half, count=2 * heads)
    pl.semaphore_wait(barrier, len(partners))
    rows_out.start()
    for copy in entry:
        copy.start()

    def pooled(which, h):
        rows = mm(small_tab[pl.ds(T_POOL, 112), pl.ds(0, 128)], rows_in[which, :, columns(h)])
        return (rows * single_tab[pl.ds(S_ANC, 112), right]).astype(BF16)

    for copy in table_loads[2:]:
        copy.wait()
    rows_out.wait_recv()

    def picked(row, count):
        return mm(half_tab[pl.ds(row, count)], rows_recv[...]).astype(BF16)

    @pl.when(core == 1)
    def _():
        for kv in (0, 1):
            far_send[:, pl.ds(128 * kv, 128)] = picked(P_COMPACT + 128 * kv, 112)
        for copy in far_copies:
            copy.start()
        far_q[...] = picked(P_FAR, 128)

    @pl.when(core == 0)
    def _():
        for kv in (0, 1):
            pair_kv[:, pl.ds(128 * kv, 128)] = picked(P_PICK + 128 * kv, 128)
        far_q[...] = picked(P_PICK + 256, 128)

    for kv in (0, 1):
        loads[kv].wait()
        entry[kv].wait_recv()

    def pool_rows(h):
        cols = columns(h)
        coarse_kv[0, :, cols] = pooled(0, h)
        coarse_kv[1, :, cols] = pooled(1, h)

    each_head(pool_rows)
    for copy in near_copies:
        copy.start()
    one_swap.start()

    loads[2].wait()
    entry[2].wait_recv()

    def pool_queries(h):
        coarse_q[:, columns(h)] = pooled(2, h)

    each_head(pool_queries)

    def to_row(column, start):
        count = column.shape[0]
        picked = column * single_tab[pl.ds(S_DIAG + start, count), everything]
        return jnp.sum(picked, axis=0, keepdims=True)

    def attend(queries, keys, vals, mask):
        scores = mm_nt(queries, keys) * SCALE
        if mask is not None:
            scores = scores + mask
        top = jnp.maximum(jnp.max(scores, axis=1, keepdims=True), FLOOR)
        weights = jnp.exp(scores - top)
        total = jnp.sum(weights, axis=1, keepdims=True)
        return weights, top, total, mm(weights.astype(BF16), vals)

    def attend_back(weights, adj, shift, queries, keys, vals):
        inner = mm_nt(adj, vals) - shift
        dscore = (weights * inner).astype(BF16)
        dkeys = mm_tn(dscore, queries) * SCALE
        return mm(dscore, keys), dkeys, mm_tn(weights.astype(BF16), adj)

    def near_rows(kv, h):
        return jnp.concatenate([near_kv[0, kv, :, columns(h)], near_kv[1, kv, :, columns(h)]], axis=0)

    def forward_all(group, start, rows, keys_of, mask, expo):
        every = range(heads)
        scores = [mm_nt(coarse_q[pl.ds(start, rows), columns(h)], keys_of(0, h)) * SCALE for h in every]
        if mask is not None:
            scores = [score + mask for score in scores]
        top = [jnp.max(score, axis=1, keepdims=True) for score in scores]
        weights = [jnp.exp(scores[h] - top[h]) for h in every]
        total = [jnp.sum(weight, axis=1, keepdims=True) for weight in weights]
        for h in every:
            expo[h] = weights[h]
            numer[h, pl.ds(start, rows)] = mm(weights[h].astype(BF16), keys_of(1, h))
        for h in every:
            tops[h, pl.ds(group, 1)] = to_row(top[h], start)
            totals[h, pl.ds(group, 1)] = to_row(total[h], start)

    def one_rows(kv, h):
        return one_kv[kv, :, columns(h)]

    def forward_one():
        forward_all(0, 0, 64, one_rows, None, expo_one)

    def forward_near():
        forward_all(1, 64, 48, near_rows, single_tab[pl.ds(S_NEAR, 48), everything], expo_near)

    def forward_far(keys, vals, mask, span):
        weights, top, total, sums = attend(far_q[...], keys, vals, mask)
        expo_far[:, pl.ds(0, span)] = weights
        lanes = lax.broadcasted_iota(jnp.int32, (128, 128), 1)
        pair = jnp.where(lanes < 64, top, total)
        whole = jnp.concatenate([sums.reshape(PLANE, 8, 128), pair.reshape(PLANE, 8, 128)], axis=1)
        sums_send[...] = whole.reshape(PLANE * 16, 128)

    @pl.when(core == 0)
    def _():
        forward_far(
            pair_kv[:, everything], pair_kv[:, right], single_tab[pl.ds(S_DIAG, 128), right], 128
        )

    @pl.when(core == 1)
    def _():
        for copy in far_copies:
            copy.wait_recv()
        forward_far(
            far_kv[:, everything], far_kv[:, right], single_tab[pl.ds(S_FAR, 128), pl.ds(0, 192)], 192
        )

    sums_back.start()

    one_swap.wait_recv()
    forward_one()
    for copy in near_copies:
        copy.wait_recv()
    share.start()

    loads[3].wait()
    entry[3].wait_recv()

    def score_local(h):
        cols = columns(h)
        local_scores[h] = mm_nt(rows_in[2, :, cols], rows_in[0, :, cols]) * SCALE
        local_dprob[h] = mm_nt(rows_in[3, :, cols], rows_in[1, :, cols])

    each_head(score_local)
    share.wait_recv()
    forward_near()
    sums_back.wait_recv()

    def combine(h):
        cols = columns(h)
        top_row = tops[h, pl.ds(0, 1)] + tops[h, pl.ds(1, 1)]
        total_row = totals[h, pl.ds(0, 1)] + totals[h, pl.ds(1, 1)]
        for group in (0, 1):
            top_row = top_row + to_row(sums_recv[h, group, pl.ds(8, 8), pl.ds(0, 1)], 112 + 8 * group)
            total_row = total_row + to_row(sums_recv[h, group, pl.ds(8, 8), pl.ds(64, 1)], 112 + 8 * group)
        scores = local_scores[h]
        coarse = single_tab[pl.ds(S_ANC, 128), everything] + top_row
        top = jnp.max(jnp.maximum(scores, coarse), axis=1, keepdims=True)
        expo = jnp.exp(scores - top)
        factor = jnp.exp(coarse - top)
        total = jnp.sum(expo + factor * total_row, axis=1, keepdims=True)
        inverse = 1.0 / total
        numer_all = jnp.concatenate(
            [numer[h], sums_recv[h, 0, pl.ds(0, 8)], sums_recv[h, 1, pl.ds(0, 8)]], axis=0
        ).astype(BF16)
        outcome = (mm(expo.astype(BF16), rows_in[1, :, cols]) + mm(factor.astype(BF16), numer_all)) * inverse
        att_buf[:, cols] = outcome.astype(BF16)
        grad = rows_in[3, :, cols]
        dots = jnp.sum(grad.astype(F32) * outcome, axis=1, keepdims=True)
        probs = expo * inverse
        weight = (factor * inverse).astype(BF16)
        local_probs[h] = probs.astype(BF16)
        local_ds[h] = (probs * (local_dprob[h] - dots)).astype(BF16)
        lane = lax.broadcasted_iota(jnp.int32, (128, 128), 1)
        dots_wide = jnp.broadcast_to(dots, (128, 128))
        dots_high = dots_wide.astype(BF16).astype(F32)
        dots_pair = jnp.where(lane < 64, dots_high, dots_wide - dots_high).astype(BF16)
        both = mm_tn(weight, jnp.concatenate([grad, dots_pair], axis=1))
        adj = both[:, 0:128]
        shift = both[:, 128:256]
        adjoint[h] = adj.astype(BF16)
        offset[h] = shift
        for group in (0, 1):
            low = 112 + 8 * group
            adj_send[h, group, pl.ds(0, 8)] = adj[low : low + 8]
            adj_send[h, group, pl.ds(8, 8)] = shift[low : low + 8]

    each_head(combine)
    adj_out.start()
    stores[0].start()
    exits[0].start()

    def shift_of(h, start, count):
        return offset[h, pl.ds(start, count), pl.ds(0, 1)] + offset[h, pl.ds(start, count), pl.ds(64, 1)]

    def backward_near(h):
        cols = columns(h)
        dqueries, dkeys, dvals = attend_back(
            expo_near[h], adjoint[h, pl.ds(64, 48)], shift_of(h, 64, 48),
            coarse_q[pl.ds(64, 48), cols], near_rows(0, h), near_rows(1, h),
        )
        dcoarse_q[h, pl.ds(64, 48)] = dqueries
        for side in (0, 1):
            part_grad[side, 0, :, cols] = dkeys[64 * side : 64 * side + 64].astype(BF16)
            part_grad[side, 1, :, cols] = dvals[64 * side : 64 * side + 64].astype(BF16)

    def backward_one(h):
        cols = columns(h)
        dqueries, dkeys, dvals = attend_back(
            expo_one[h], adjoint[h, pl.ds(0, 64)], shift_of(h, 0, 64),
            coarse_q[pl.ds(0, 64), cols], one_kv[0, :, cols], one_kv[1, :, cols],
        )
        dcoarse_q[h, pl.ds(0, 64)] = dqueries
        one_part[0, :, cols] = dkeys.astype(BF16)
        one_part[1, :, cols] = dvals.astype(BF16)

    each_head(backward_near)
    part_swap.start()
    each_head(backward_one)
    one_back.start()

    def unpooled(rows):
        count = rows.shape[0]
        scaled = rows * single_tab[pl.ds(S_ANC, count), right]
        return mm(small_tab[pl.ds(T_POOL, 128), pl.ds(128, count)], scaled.astype(BF16))

    def query_total(h):
        cols = columns(h)
        total = mm(local_ds[h], rows_in[0, :, cols]) + unpooled(dcoarse_q[h])
        dquery_buf[:, cols] = (total * SCALE).astype(BF16)

    each_head(query_total)
    stores[1].start()
    exits[1].start()
    part_swap.wait_recv()

    def sum_near(h):
        cols = columns(h)
        for kv in (0, 1):
            both = part_grad[0, kv, :, cols].astype(F32) + swap_grad[kv, :, cols].astype(F32)
            send_grad[kv, :, cols] = both.astype(BF16)

    each_head(sum_near)
    for copy in near_back:
        copy.start()
    one_back.wait_recv()

    def local_back(h):
        cols = columns(h)
        dkeys = mm_tn(local_ds[h], rows_in[2, :, cols]) * SCALE
        dvals = mm_tn(local_probs[h], rows_in[3, :, cols])
        for kv, total in ((0, dkeys), (1, dvals)):
            total = total + unpooled(one_recv[kv, :, cols].astype(F32))
            dkv_buf[kv, :, cols] = total.astype(BF16)

    each_head(local_back)
    for i in (2, 3):
        stores[i].start()
        exits[i].start()

    adj_out.wait_recv()

    def backward_far(keys, vals, span):
        arrived = adj_recv[...].reshape(PLANE, 16, 128)
        adj = arrived[:, 0:8].reshape(128, 128).astype(BF16)
        shift = arrived[:, 8:16].reshape(128, 128)
        shift = shift[:, 0:1] + shift[:, 64:65]
        dqueries, dkeys, dvals = attend_back(expo_far[:, pl.ds(0, span)], adj, shift, far_q[...], keys, vals)
        return (dqueries * SCALE).astype(BF16), dkeys.astype(BF16), dvals.astype(BF16)

    @pl.when(core == 0)
    def _():
        dqueries, dkeys, dvals = backward_far(pair_kv[:, everything], pair_kv[:, right], 128)
        rows = jnp.concatenate([dkeys, dvals, dqueries], axis=0)
        drows_send[...] = mm(place_tab[:, pl.ds(P_PICK, 384)], rows).astype(BF16)

    @pl.when(core == 1)
    def _():
        dqueries, dkeys, dvals = backward_far(far_kv[:, everything], far_kv[:, right], 192)
        dfar_send[:, everything] = dkeys
        dfar_send[:, right] = dvals
        for copy in far_back:
            copy.start()
        dfar_q[...] = dqueries
        for copy in far_back:
            copy.wait_recv()
        came = dfar_recv[...].astype(F32)
        level_six = came[64:96] + came[96:128]
        level_seven = (came[128:144] + came[144:160]) + (came[160:176] + came[176:192])
        rows = jnp.concatenate([came[0:64], level_six, level_seven, jnp.zeros((16, 256), F32)], axis=0).astype(BF16)
        rows = jnp.concatenate([dfar_q[...], rows[:, 0:128], rows[:, 128:256]], axis=0)
        drows_send[...] = mm(place_tab[:, pl.ds(P_FAR, 384)], rows).astype(BF16)

    drows_back.start()

    for copy in near_back:
        copy.wait_recv()

    def gather_coarse(h):
        cols = columns(h)
        for kv in (0, 1):
            coarse = jnp.concatenate(
                [
                    recv_grad[kv, pl.ds(0, 32), cols].astype(F32),
                    recv_grad[kv, pl.ds(32, 16), cols].astype(F32)
                    + recv_grad[kv, pl.ds(48, 16), cols].astype(F32),
                ],
                axis=0,
            )
            total = mm(small_tab[pl.ds(T_GATHER, 32), pl.ds(0, 48)], coarse.astype(BF16)).astype(BF16)
            coarse_grad[0, pl.ds(16 * kv, 16), cols] = total[0:16]
            coarse_grad[1, pl.ds(16 * kv, 16), cols] = total[16:32]

    each_head(gather_coarse)
    coarse_store.start()
    coarse_exit.start()
    drows_back.wait_recv()

    for copy in entry + near_copies + near_back + [one_swap, share, part_swap, one_back, coarse_exit] + exits:
        copy.wait_send()
    for copy in (rows_out, sums_back, adj_out, drows_back):
        copy.wait_send()

    @pl.when(core == 1)
    def _():
        for copy in far_copies + far_back:
            copy.wait_send()

    for copy in stores + [coarse_store]:
        copy.wait()
    for copy in exit_waits + [coarse_wait]:
        copy.wait_recv()


def last_kernel(
    heads, att_ref, dquery_ref, dkey_ref, dvalue_ref, coarse_ref, far_ref, att_out, dquery_out, dkey_out, dvalue_out
):
    att_out[...] = att_ref[...]
    rows = lax.broadcasted_iota(jnp.int32, (64, 32), 0)
    parents = lax.broadcasted_iota(jnp.int32, (64, 32), 1)

    def among(first, count, span):
        at = parents - first
        return (at >= 0) & (at < count) & (rows >= span * at) & (rows < span * at + span)

    spread = jnp.where(among(0, 16, 4), 0.5, 0.0).astype(BF16)[:, 0:16]
    far = [
        jnp.where(among(4 * x, 4, 16), 0.25, 0.0)
        + jnp.where(among(16 + 4 * x, 2, 32), 2.0**-2.5, 0.0)
        + jnp.where(among(18 + 4 * x, 1, 64), 2.0**-3, 0.0)
        + jnp.where(among(19 + 4 * x, 1, 64), 2.0**-3.5, 0.0)
        for x in range(3)
    ]
    far = jnp.concatenate(far, axis=0).astype(BF16)
    for h in range(heads):
        cols = pl.ds(DH * h, DH)
        added = mm(far, far_ref[pl.ds(32 * h, 32)])
        near = [mm(spread, coarse_ref[pl.ds(16 * kv, 16), cols]) for kv in (0, 1)]
        dkey_out[:, cols] = (dkey_ref[:, cols].astype(F32) + added[0:64] + near[0]).astype(BF16)
        dvalue_out[:, cols] = (dvalue_ref[:, cols].astype(F32) + added[64:128] + near[1]).astype(BF16)
        dquery_out[:, cols] = (dquery_ref[:, cols].astype(F32) + added[128:192]).astype(BF16)


def solution(mesh):
    small, halves, places, singles = tables()
    small, halves, places = (table.astype(BF16) for table in (small, halves, places))

    def local(queries, key_rows, values, out_grad):
        rows, columns = queries.shape
        width = columns // 2
        heads = width // DH
        tall = 2 * rows
        anywhere = pl.BlockSpec(memory_space=pl.ANY)
        out = jax.ShapeDtypeStruct((rows, columns), BF16)
        vmem = pltpu.VMEM
        scratch = [
            vmem((192, 256), BF16),
            vmem((768, 512), BF16),
            vmem((512, 768), BF16),
            vmem((S_ROWS, 256), F32),
            vmem((3 * rows, columns), BF16),
            vmem((4, tall, width), BF16),
            vmem((2, 112, width), BF16),
            vmem((112, width), BF16),
            vmem((2, 64, width), BF16),
            vmem((2, 2, 64, width), BF16),
            vmem((2 * heads, 2, 16, 128), BF16),
            vmem((PLANE * 32, 128), BF16),
            vmem((128, 128), BF16),
            vmem((112, 256), BF16),
            vmem((192, 256), BF16),
            vmem((128, 256), BF16),
            vmem((heads, 128, 128), F32),
            vmem((heads, 128, 128), F32),
            vmem((heads, 64, 64), F32),
            vmem((heads, 48, 128), F32),
            vmem((128, 192), F32),
            vmem((heads, 112, 128), F32),
            vmem((heads, 8, 128), F32),
            vmem((heads, 8, 128), F32),
            vmem((PLANE * 16, 128), F32),
            vmem((heads, 2, 16, 128), F32),
            vmem((heads, 2, 16, 128), F32),
            vmem((PLANE * 16, 128), F32),
            vmem((128, 128), BF16),
            vmem((PLANE * 32, 128), BF16),
            vmem((192, 256), BF16),
            vmem((192, 256), BF16),
            vmem((tall, width), BF16),
            vmem((tall, width), BF16),
            vmem((2, tall, width), BF16),
            vmem((heads, 128, 128), BF16),
            vmem((heads, 128, 128), BF16),
            vmem((heads, 128, 128), BF16),
            vmem((heads, 128, 128), F32),
            vmem((heads, 112, 128), F32),
            vmem((2, 2, 64, width), BF16),
            vmem((2, 64, width), BF16),
            vmem((2, 64, width), BF16),
            vmem((2, 64, width), BF16),
            vmem((2, 64, width), BF16),
            vmem((2, 64, width), BF16),
            vmem((2, 32, width), BF16),
            pltpu.SemaphoreType.DMA((11,)),
            pltpu.SemaphoreType.DMA((5,)),
            pltpu.SemaphoreType.DMA((4,)),
            pltpu.SemaphoreType.DMA((COPIES,)),
            pltpu.SemaphoreType.DMA((COPIES,)),
        ]
        parts = pl.pallas_call(
            functools.partial(kernel, heads),
            out_shape=(out,) * 4
            + (jax.ShapeDtypeStruct((32, columns), BF16), jax.ShapeDtypeStruct((64 * heads, 128), BF16)),
            in_specs=[anywhere] * 8,
            out_specs=(anywhere,) * 6,
            scratch_shapes=scratch,
            compiler_params=pltpu.CompilerParams(
                collective_id=0, has_side_effects=True, vmem_limit_bytes=60 << 20
            ),
            name="sibling_attention",
        )(key_rows, values, queries, out_grad, *(jnp.asarray(table) for table in (small, halves, places, singles)))
        whole = pl.BlockSpec(memory_space=pltpu.VMEM)
        return pl.pallas_call(
            functools.partial(last_kernel, 2 * heads),
            out_shape=(out,) * 4,
            in_specs=[whole] * 6,
            out_specs=(whole,) * 4,
            name="coarse_rows_added",
        )(*parts)

    spec = P(("seq", "head"), None)
    return jax.shard_map(
        local, mesh=mesh, in_specs=(spec,) * 4, out_specs=(spec,) * 4, check_vma=False
    )
```

```python
import functools
import math

import jax
import jax.numpy as jnp
import numpy as np
from jax import lax
from jax.experimental import pallas as pl
from jax.experimental.pallas import tpu as pltpu
from jax.sharding import PartitionSpec as P

MESH = pl.DeviceIdType.MESH
BF16 = jnp.bfloat16
F32 = jnp.float32
DH = 128
SCALE = 1.0 / math.sqrt(DH)
LOW = -1e30
FLOOR = -1e29

NEAR = ((1, 64, 0, 32), (2, 96, 32, 16), (3, 96, 48, 16))
FAR = ((1, 0, 0, 64), (2, 64, 64, 32), (3, 64, 96, 32))
FAR += tuple((n, 96, 128 + 16 * (n - 4), 16) for n in (4, 5, 6, 7))
PLANE = 16
PACK = 4


def tables():
    level_of = np.zeros(128, np.int64)
    pool = np.zeros((128, 128), np.float32)
    row = 0
    for level in range(1, 8):
        for i in range(128 >> level):
            pool[row, i << level : (i + 1) << level] = 1.0
            level_of[row] = level
            row += 1
    level_of[127] = 99
    pick = np.zeros((3, 128, 512), np.float32)
    pick_far = np.zeros((128, 512), np.float32)
    compact = np.zeros((2, 128, 512), np.float32)
    for i in range(PLANE):
        for half in range(2):
            at = 32 * i + 16 * half
            for x in range(3):
                for r in range(4):
                    pick[x, 8 * i + 4 * half + r, at + 4 * x + r] = 1.0
            for r in range(2):
                pick_far[8 * i + 2 * half + r, at + 8 + r] = 1.0
            pick_far[8 * i + 4 + half, at + 10] = 1.0
            pick_far[8 * i + 6, at + 11] = 1.0
            for kv in range(2):
                for r in range(2):
                    compact[kv, 4 * i + 2 * half + r, at + 4 * kv + r] = 1.0
                compact[kv, 64 + 2 * i + half, at + 4 * kv + 2] = 1.0
                compact[kv, 96 + i, at + 4 * kv + 3] = 1.0
    blocks = [pick[0], pick[1], pick[2], pick_far, compact[0], compact[1]]
    halves = np.concatenate(blocks, axis=0)
    places = np.concatenate([block.T for block in blocks], axis=1)
    small = np.zeros((192, 256), np.float32)
    small[0:128, :128] = pool
    small[0:128, 128:256] = pool.T
    for x in range(3):
        for r in range(4):
            small[128 + 4 * x + r, 64 * x + 16 * r : 64 * x + 16 * r + 16] = 1.0
        for r in range(2):
            small[144 + 4 * x + r, 64 * x + 32 * r : 64 * x + 32 * r + 32] = 1.0
        small[146 + 4 * x : 148 + 4 * x, 64 * x : 64 * x + 64] = 1.0
    for r in range(32):
        small[160 + r, r] = 1.0
        small[160 + r, 32 + r // 2] = 2.0**-0.5
    ancestor = np.where(pool.T > 0, 0.0, LOW)
    row_scale = np.where(level_of < 8, 2.0 ** (-level_of / 2.0), 0.0)[:, None] * np.ones((1, 128))
    half_scale = 2.0 ** (-np.array([4] * 16 + [5, 5, 6, 7] * 4) / 2.0)
    shard = np.arange(128) // 8
    across = np.where(shard[:, None] // 8 != shard[None, :] // 8, 0.0, LOW)
    near = np.full((48, 256), LOW)
    for r in range(48):
        for k in range(128):
            if level_of[64 + r] == (2 if k % 64 < 32 else 3):
                near[r, k] = 0.0
    far = np.full((128, 256), LOW)
    for r in range(128):
        for k in range(192):
            if level_of[120 + r % 8] == 5 + k // 64:
                far[r, k] = 0.0
    singles = np.concatenate(
        [
            np.concatenate([ancestor, row_scale], axis=1),
            np.concatenate([np.eye(128), across], axis=1),
            np.repeat(half_scale[:, None], 256, axis=1),
            near,
            far,
        ],
        axis=0,
    )
    return small, halves, places, singles.astype(np.float32)


T_POOL, T_HALF, T_GATHER = 0, 128, 160
P_PICK, P_FAR, P_COMPACT = 0, 384, 512
S_ANC, S_DIAG, S_HALF, S_NEAR, S_FAR = 0, 128, 256, 288, 336
S_ROWS = 464

C_ENTRY, C_EXIT, C_ONE, C_SHARE, C_PART, C_ONE_BACK = 0, 4, 8, 9, 10, 11
C_NEAR, C_NEAR_BACK, C_FAR, C_FAR_BACK = 11, 14, 17, 24
C_ROWS, C_SUMS, C_ADJ, C_DROWS, C_COARSE = 32, 64, 80, 96, 128
COPIES = 129


def mm(a, b):
    return lax.dot_general(a, b, (((1,), (0,)), ((), ())), preferred_element_type=F32)


def mm_nt(a, b):
    return lax.dot_general(a, b, (((1,), (1,)), ((), ())), preferred_element_type=F32)


def mm_tn(a, b):
    return lax.dot_general(a, b, (((0,), (0,)), ((), ())), preferred_element_type=F32)


def flipped(index, mask):
    for bit in range(8):
        if mask >> bit & 1:
            own = lax.rem(lax.div(index, 1 << bit), 2)
            index = index + (1 << bit) * (1 - 2 * own)
    return index


def kernel(
    heads,
    key_hbm, value_hbm, query_hbm, grad_hbm, small_hbm, half_hbm, place_hbm, single_hbm,
    att_hbm, dquery_hbm, dkey_hbm, dvalue_hbm, coarse_hbm, far_hbm,
    small_tab, half_tab, place_tab, single_tab, raw_in, rows_in, coarse_kv, coarse_q, one_kv, near_kv,
    rows_send, rows_recv, far_q, far_send, far_kv, pair_kv,
    local_scores, local_dprob, expo_one, expo_near, expo_far, numer, tops, totals,
    sums_send, sums_recv, adj_send, adj_recv, dfar_q, drows_send,
    dfar_send, dfar_recv,
    att_buf, dquery_buf, dkv_buf, local_ds, local_probs, adjoint, offset, dcoarse_q,
    part_grad, swap_grad, send_grad, recv_grad, one_part, one_recv, coarse_grad,
    load_sem, store_sem, self_sem, send_sem, recv_sem,
):
    seq = lax.axis_index("seq")
    head = lax.axis_index("head")
    width = heads * DH
    core = lax.rem(seq, 2)
    place = lax.rem(seq, PLANE)
    chip = lax.div(place, 2)
    mate = (seq, 1 - head)
    twin = (flipped(seq, 1), head)
    near_dev = {n: (flipped(seq, n << 1), head) for n, _, _, _ in NEAR}
    far_dev = {n: (flipped(seq, n << 4), head) for n, _, _, _ in FAR}
    peers = []
    for m in range(PLANE):
        there = flipped(seq, m)
        slot = lax.rem(there, PLANE)
        peers.append(((there, head), slot, lax.div(slot, 2), lax.rem(slot, 2)))
    mine = pl.ds(pl.multiple_of(head * width, width), width)
    theirs = pl.ds(pl.multiple_of((1 - head) * width, width), width)
    sources = (key_hbm, value_hbm, query_hbm, grad_hbm)

    def remote(src, dst, slot, device):
        return pltpu.make_async_remote_copy(
            src_ref=src, dst_ref=dst, send_sem=send_sem.at[slot], recv_sem=recv_sem.at[slot],
            device_id=device, device_id_type=MESH,
        )

    def slab(slot, rows):
        return pl.ds(pl.multiple_of(slot * rows, rows), rows)

    loads = [
        pltpu.make_async_copy(ref.at[:, mine], rows_in.at[i, pl.ds(0, 64)], load_sem.at[i])
        for i, ref in enumerate(sources)
    ]
    table_loads = [
        pltpu.make_async_copy(small_hbm, small_tab, load_sem.at[4]),
        pltpu.make_async_copy(single_hbm, single_tab, load_sem.at[5]),
        pltpu.make_async_copy(half_hbm, half_tab, load_sem.at[9]),
        pltpu.make_async_copy(place_hbm, place_tab, load_sem.at[10]),
    ]
    raw_loads = [
        pltpu.make_async_copy(ref, raw_in.at[pl.ds(64 * i, 64)], load_sem.at[6 + i]) for i, ref in enumerate(sources[:3])
    ]
    coarse_store = pltpu.make_async_copy(coarse_grad.at[0], coarse_hbm.at[:, mine], store_sem.at[4])
    coarse_exit = remote(coarse_grad.at[1], coarse_hbm.at[:, mine], C_COARSE, mate)
    coarse_wait = remote(coarse_grad.at[1], coarse_hbm.at[:, theirs], C_COARSE, mate)
    entry = [
        remote(ref.at[:, theirs], rows_in.at[i, pl.ds(64, 64)], C_ENTRY + i, mate)
        for i, ref in enumerate(sources)
    ]
    one_swap = remote(coarse_kv.at[:, pl.ds(0, 64)], one_kv, C_ONE, twin)
    near_copies = [
        remote(coarse_kv.at[:, pl.ds(src, count)], near_kv.at[0, :, pl.ds(dst, count)], C_NEAR + n, near_dev[n])
        for n, src, dst, count in NEAR
    ]
    share = remote(near_kv.at[0], near_kv.at[1], C_SHARE, twin)
    far_copies = [
        remote(far_send.at[pl.ds(src, count)], far_kv.at[pl.ds(dst, count)], C_FAR + n, far_dev[n])
        for n, src, dst, count in FAR
    ]
    far_back = [
        remote(dfar_send.at[pl.ds(dst, count)], dfar_recv.at[pl.ds(dst, count)], C_FAR_BACK + n, far_dev[n])
        for n, _, dst, count in FAR
    ]
    part_swap = remote(part_grad.at[1], swap_grad, C_PART, twin)
    near_back = [
        remote(send_grad.at[:, pl.ds(dst, count)], recv_grad.at[:, pl.ds(dst, count)], C_NEAR_BACK + n, near_dev[n])
        for n, _, dst, count in NEAR
    ]
    one_back = remote(one_part, one_recv, C_ONE_BACK, twin)

    class Spread:
        def __init__(self, which, base, send, recv, rows):
            self.local = pltpu.make_async_copy(
                send.at[chip, core], recv.at[slab(place, rows)], self_sem.at[which]
            )
            self.out = []
            self.come = []
            for m in range(1, PLANE):
                device, slot, owner, group = peers[m]
                self.out.append(remote(send.at[owner, group], recv.at[slab(place, rows)], base + m, device))
                self.come.append(remote(send.at[owner, group], recv.at[slab(slot, rows)], base + m, device))

        def start(self):
            for copy in self.out:
                copy.start()
            self.local.start()

        def wait_recv(self):
            self.local.wait()
            for copy in self.come:
                copy.wait_recv()

        def wait_send(self):
            for copy in self.out:
                copy.wait_send()

    class Return(Spread):
        def __init__(self, which, base, send, recv, rows):
            self.local = pltpu.make_async_copy(
                send.at[slab(place, rows)], recv.at[chip, core], self_sem.at[which]
            )
            self.out = []
            self.come = []
            for m in range(1, PLANE):
                device, slot, owner, group = peers[m]
                self.out.append(remote(send.at[slab(slot, rows)], recv.at[chip, core], base + m, device))
                self.come.append(remote(send.at[slab(slot, rows)], recv.at[owner, group], base + m, device))

    class Rows:
        def __init__(self, which, base, pairs):
            self.local = pltpu.make_async_copy(*pairs(0, 0)[:2], self_sem.at[which])
            self.out = []
            self.come = []
            for side in (0, 1):
                for m in range(PLANE):
                    if side == 0 and m == 0:
                        continue
                    src, dst, land = pairs(side, m)
                    device = (peers[m][0][0], mate[1] if side else head)
                    self.out.append(remote(src, dst, base + 16 * side + m, device))
                    self.come.append(remote(src, land, base + 16 * side + m, device))

        start = Spread.start
        wait_recv = Spread.wait_recv
        wait_send = Spread.wait_send

    def message_pairs(side, m):
        _, slot, owner, group = peers[m]
        group_of_heads = mate[1] if side else head
        return (
            rows_send.at[group_of_heads * heads + owner, group],
            rows_recv.at[slab(2 * place + side, 16)],
            rows_recv.at[slab(2 * slot + side, 16)],
        )

    def drow_pairs(side, m):
        _, slot, owner, group = peers[m]
        group_of_heads = mate[1] if side else head
        return (
            drows_send.at[slab(2 * slot + side, 16)],
            far_hbm.at[slab(2 * (head * heads + chip) + core, 16)],
            far_hbm.at[slab(2 * (group_of_heads * heads + owner) + group, 16)],
        )

    rows_out = Rows(0, C_ROWS, message_pairs)
    sums_back = Return(1, C_SUMS, sums_send, sums_recv, 16)
    adj_out = Spread(2, C_ADJ, adj_send, adj_recv, 16)
    drows_back = Rows(3, C_DROWS, drow_pairs)

    results = ((att_buf, att_hbm), (dquery_buf, dquery_hbm), (dkv_buf.at[0], dkey_hbm), (dkv_buf.at[1], dvalue_hbm))
    stores = [
        pltpu.make_async_copy(buf.at[pl.ds(0, 64)], out.at[:, mine], store_sem.at[i])
        for i, (buf, out) in enumerate(results)
    ]
    exits = [
        remote(buf.at[pl.ds(64, 64)], out.at[:, mine], C_EXIT + i, mate)
        for i, (buf, out) in enumerate(results)
    ]
    exit_waits = [
        remote(buf.at[pl.ds(64, 64)], out.at[:, theirs], C_EXIT + i, mate)
        for i, (buf, out) in enumerate(results)
    ]

    for copy in raw_loads + table_loads + loads:
        copy.start()
    barrier = pltpu.get_barrier_semaphore()
    partners = [peer[0] for peer in peers[1:]] + [(peer[0][0], mate[1]) for peer in peers] + list(far_dev.values())
    for device in partners:
        pl.semaphore_signal(barrier, inc=1, device_id=device, device_id_type=MESH)
    def columns(h):
        return pl.ds(h * DH, DH)

    def each_head(*steps, count=heads):
        for step in steps:
            for h in range(count):
                step(h)

    for copy in table_loads[:2]:
        copy.wait()
    everything = pl.ds(0, 128)
    right = pl.ds(128, 128)

    for copy in raw_loads:
        copy.wait()

    def pool_half(h):
        rows = mm(small_tab[pl.ds(T_HALF, 32), pl.ds(0, 192)], raw_in[:, columns(h)])
        rows = (rows * single_tab[pl.ds(S_HALF, 32), everything]).astype(BF16)
        rows_send[h, 0] = rows[0:16]
        rows_send[h, 1] = rows[16:32]

    each_head(pool_half, count=2 * heads)
    pl.semaphore_wait(barrier, len(partners))
    rows_out.start()
    for copy in entry:
        copy.start()

    def pooled(which, h):
        rows = mm(small_tab[pl.ds(T_POOL, 112), pl.ds(0, 128)], rows_in[which, :, columns(h)])
        return (rows * single_tab[pl.ds(S_ANC, 112), right]).astype(BF16)

    for copy in table_loads[2:]:
        copy.wait()
    rows_out.wait_recv()

    def picked(row, count):
        return mm(half_tab[pl.ds(row, count)], rows_recv[...]).astype(BF16)

    @pl.when(core == 1)
    def _():
        for kv in (0, 1):
            far_send[:, pl.ds(128 * kv, 128)] = picked(P_COMPACT + 128 * kv, 112)
        for copy in far_copies:
            copy.start()
        far_q[...] = picked(P_FAR, 128)

    @pl.when(core == 0)
    def _():
        for kv in (0, 1):
            pair_kv[:, pl.ds(128 * kv, 128)] = picked(P_PICK + 128 * kv, 128)
        far_q[...] = picked(P_PICK + 256, 128)

    for kv in (0, 1):
        loads[kv].wait()
        entry[kv].wait_recv()

    def pool_rows(h):
        cols = columns(h)
        coarse_kv[0, :, cols] = pooled(0, h)
        coarse_kv[1, :, cols] = pooled(1, h)

    each_head(pool_rows)
    for copy in near_copies:
        copy.start()
    one_swap.start()

    loads[2].wait()
    entry[2].wait_recv()

    def pool_queries(h):
        coarse_q[:, columns(h)] = pooled(2, h)

    each_head(pool_queries)

    def to_row(column, start):
        count = column.shape[0]
        picked = column * single_tab[pl.ds(S_DIAG + start, count), everything]
        return jnp.sum(picked, axis=0, keepdims=True)

    def attend(queries, keys, vals, mask):
        scores = mm_nt(queries, keys) * SCALE
        if mask is not None:
            scores = scores + mask
        top = jnp.maximum(jnp.max(scores, axis=1, keepdims=True), FLOOR)
        weights = jnp.exp(scores - top)
        total = jnp.sum(weights, axis=1, keepdims=True)
        return weights, top, total, mm(weights.astype(BF16), vals)

    def attend_back(weights, adj, shift, queries, keys, vals):
        inner = mm_nt(adj, vals) - shift
        dscore = (weights * inner).astype(BF16)
        dkeys = mm_tn(dscore, queries) * SCALE
        return mm(dscore, keys), dkeys, mm_tn(weights.astype(BF16), adj)

    def near_rows(kv, h):
        return jnp.concatenate([near_kv[0, kv, :, columns(h)], near_kv[1, kv, :, columns(h)]], axis=0)

    def forward_all(group, start, rows, keys_of, mask, expo):
        every = range(heads)
        scores = [mm_nt(coarse_q[pl.ds(start, rows), columns(h)], keys_of(0, h)) * SCALE for h in every]
        if mask is not None:
            scores = [score + mask for score in scores]
        top = [jnp.max(score, axis=1, keepdims=True) for score in scores]
        weights = [jnp.exp(scores[h] - top[h]) for h in every]
        total = [jnp.sum(weight, axis=1, keepdims=True) for weight in weights]
        for h in every:
            expo[h] = weights[h]
            numer[h, pl.ds(start, rows)] = mm(weights[h].astype(BF16), keys_of(1, h))
        for h in every:
            tops[h, pl.ds(group, 1)] = to_row(top[h], start)
            totals[h, pl.ds(group, 1)] = to_row(total[h], start)

    def one_rows(kv, h):
        return one_kv[kv, :, columns(h)]

    def forward_one():
        forward_all(0, 0, 64, one_rows, None, expo_one)

    def forward_near():
        forward_all(1, 64, 48, near_rows, single_tab[pl.ds(S_NEAR, 48), everything], expo_near)

    def forward_far(keys, vals, mask, span):
        weights, top, total, sums = attend(far_q[...], keys, vals, mask)
        expo_far[:, pl.ds(0, span)] = weights
        lanes = lax.broadcasted_iota(jnp.int32, (128, 128), 1)
        pair = jnp.where(lanes < 64, top, total)
        whole = jnp.concatenate([sums.reshape(PLANE, 8, 128), pair.reshape(PLANE, 8, 128)], axis=1)
        sums_send[...] = whole.reshape(PLANE * 16, 128)

    @pl.when(core == 0)
    def _():
        forward_far(
            pair_kv[:, everything], pair_kv[:, right], single_tab[pl.ds(S_DIAG, 128), right], 128
        )

    @pl.when(core == 1)
    def _():
        for copy in far_copies:
            copy.wait_recv()
        forward_far(
            far_kv[:, everything], far_kv[:, right], single_tab[pl.ds(S_FAR, 128), pl.ds(0, 192)], 192
        )

    sums_back.start()

    one_swap.wait_recv()
    forward_one()
    for copy in near_copies:
        copy.wait_recv()
    share.start()

    loads[3].wait()
    entry[3].wait_recv()

    def score_local(h):
        cols = columns(h)
        local_scores[h] = mm_nt(rows_in[2, :, cols], rows_in[0, :, cols]) * SCALE
        local_dprob[h] = mm_nt(rows_in[3, :, cols], rows_in[1, :, cols])

    each_head(score_local)
    share.wait_recv()
    forward_near()
    sums_back.wait_recv()

    def combine(every):
        lane = lax.broadcasted_iota(jnp.int32, (128, 128), 1)
        coarse = {}
        total_row = {}
        for h in every:
            top_row = tops[h, pl.ds(0, 1)] + tops[h, pl.ds(1, 1)]
            totals_row = totals[h, pl.ds(0, 1)] + totals[h, pl.ds(1, 1)]
            for group in (0, 1):
                top_row = top_row + to_row(sums_recv[h, group, pl.ds(8, 8), pl.ds(0, 1)], 112 + 8 * group)
                totals_row = totals_row + to_row(sums_recv[h, group, pl.ds(8, 8), pl.ds(64, 1)], 112 + 8 * group)
            coarse[h] = single_tab[pl.ds(S_ANC, 128), everything] + top_row
            total_row[h] = totals_row
        top = {h: jnp.max(jnp.maximum(local_scores[h], coarse[h]), axis=1, keepdims=True) for h in every}
        expo = {h: jnp.exp(local_scores[h] - top[h]) for h in every}
        factor = {h: jnp.exp(coarse[h] - top[h]) for h in every}
        inverse = {h: 1.0 / jnp.sum(expo[h] + factor[h] * total_row[h], axis=1, keepdims=True) for h in every}
        outcome = {}
        for h in every:
            numer_all = jnp.concatenate(
                [numer[h], sums_recv[h, 0, pl.ds(0, 8)], sums_recv[h, 1, pl.ds(0, 8)]], axis=0
            ).astype(BF16)
            sums = mm(expo[h].astype(BF16), rows_in[1, :, columns(h)]) + mm(factor[h].astype(BF16), numer_all)
            outcome[h] = sums * inverse[h]
        dots = {}
        for h in every:
            att_buf[:, columns(h)] = outcome[h].astype(BF16)
            dots[h] = jnp.sum(rows_in[3, :, columns(h)].astype(F32) * outcome[h], axis=1, keepdims=True)
        for h in every:
            dots_wide = jnp.broadcast_to(dots[h], (128, 128))
            dots_high = dots_wide.astype(BF16).astype(F32)
            dots_pair = jnp.where(lane < 64, dots_high, dots_wide - dots_high).astype(BF16)
            weight = (factor[h] * inverse[h]).astype(BF16)
            both = mm_tn(weight, jnp.concatenate([rows_in[3, :, columns(h)], dots_pair], axis=1))
            adj = both[:, 0:128]
            shift = both[:, 128:256]
            adjoint[h] = adj.astype(BF16)
            offset[h] = shift
            for group in (0, 1):
                low = 112 + 8 * group
                adj_send[h, group, pl.ds(0, 8)] = adj[low : low + 8]
                adj_send[h, group, pl.ds(8, 8)] = shift[low : low + 8]
        for h in every:
            probs = expo[h] * inverse[h]
            local_probs[h] = probs.astype(BF16)
            local_ds[h] = (probs * (local_dprob[h] - dots[h])).astype(BF16)

    for first in range(0, heads, PACK):
        combine(range(first, min(first + PACK, heads)))
    adj_out.start()
    stores[0].start()
    exits[0].start()

    def shift_of(h, start, count):
        return offset[h, pl.ds(start, count), pl.ds(0, 1)] + offset[h, pl.ds(start, count), pl.ds(64, 1)]

    def backward_all(start, rows, keys_of, expo, put):
        every = range(heads)
        queries = [coarse_q[pl.ds(start, rows), columns(h)] for h in every]
        inner = [
            mm_nt(adjoint[h, pl.ds(start, rows)], keys_of(1, h)) - shift_of(h, start, rows) for h in every
        ]
        dscore = [(expo[h] * inner[h]).astype(BF16) for h in every]
        dqueries = [mm(dscore[h], keys_of(0, h)) for h in every]
        dkeys = [mm_tn(dscore[h], queries[h]) * SCALE for h in every]
        dvals = [mm_tn(expo[h].astype(BF16), adjoint[h, pl.ds(start, rows)]) for h in every]
        for h in every:
            dcoarse_q[h, pl.ds(start, rows)] = dqueries[h]
            put(h, 0, dkeys[h].astype(BF16))
            put(h, 1, dvals[h].astype(BF16))

    def backward_near():
        def put(h, kv, rows):
            part_grad[0, kv, :, columns(h)] = rows[0:64]
            part_grad[1, kv, :, columns(h)] = rows[64:128]

        backward_all(64, 48, near_rows, expo_near, put)

    def backward_one():
        def put(h, kv, rows):
            one_part[kv, :, columns(h)] = rows

        backward_all(0, 64, one_rows, expo_one, put)

    backward_near()
    part_swap.start()
    backward_one()
    one_back.start()

    def unpooled(rows):
        count = rows.shape[0]
        scaled = rows * single_tab[pl.ds(S_ANC, count), right]
        return mm(small_tab[pl.ds(T_POOL, 128), pl.ds(128, count)], scaled.astype(BF16))

    def query_total(h):
        cols = columns(h)
        total = mm(local_ds[h], rows_in[0, :, cols]) + unpooled(dcoarse_q[h])
        dquery_buf[:, cols] = (total * SCALE).astype(BF16)

    each_head(query_total)
    stores[1].start()
    exits[1].start()
    part_swap.wait_recv()

    def sum_near(h):
        cols = columns(h)
        for kv in (0, 1):
            both = part_grad[0, kv, :, cols].astype(F32) + swap_grad[kv, :, cols].astype(F32)
            send_grad[kv, :, cols] = both.astype(BF16)

    each_head(sum_near)
    for copy in near_back:
        copy.start()
    adj_out.wait_recv()

    def backward_far(keys, vals, span):
        arrived = adj_recv[...].reshape(PLANE, 16, 128)
        adj = arrived[:, 0:8].reshape(128, 128).astype(BF16)
        shift = arrived[:, 8:16].reshape(128, 128)
        shift = shift[:, 0:1] + shift[:, 64:65]
        dqueries, dkeys, dvals = attend_back(expo_far[:, pl.ds(0, span)], adj, shift, far_q[...], keys, vals)
        return (dqueries * SCALE).astype(BF16), dkeys.astype(BF16), dvals.astype(BF16)

    @pl.when(core == 0)
    def _():
        dqueries, dkeys, dvals = backward_far(pair_kv[:, everything], pair_kv[:, right], 128)
        rows = jnp.concatenate([dkeys, dvals, dqueries], axis=0)
        drows_send[...] = mm(place_tab[:, pl.ds(P_PICK, 384)], rows).astype(BF16)
        drows_back.start()

    @pl.when(core == 1)
    def _():
        dqueries, dkeys, dvals = backward_far(far_kv[:, everything], far_kv[:, right], 192)
        dfar_send[:, everything] = dkeys
        dfar_send[:, right] = dvals
        for copy in far_back:
            copy.start()
        dfar_q[...] = dqueries

    one_back.wait_recv()

    def local_back(h):
        cols = columns(h)
        dkeys = mm_tn(local_ds[h], rows_in[2, :, cols]) * SCALE
        dvals = mm_tn(local_probs[h], rows_in[3, :, cols])
        for kv, total in ((0, dkeys), (1, dvals)):
            total = total + unpooled(one_recv[kv, :, cols].astype(F32))
            dkv_buf[kv, :, cols] = total.astype(BF16)

    each_head(local_back)
    for i in (2, 3):
        stores[i].start()
        exits[i].start()

    @pl.when(core == 1)
    def _():
        for copy in far_back:
            copy.wait_recv()
        came = dfar_recv[...].astype(F32)
        level_six = came[64:96] + came[96:128]
        level_seven = (came[128:144] + came[144:160]) + (came[160:176] + came[176:192])
        rows = jnp.concatenate([came[0:64], level_six, level_seven, jnp.zeros((16, 256), F32)], axis=0).astype(BF16)
        rows = jnp.concatenate([dfar_q[...], rows[:, 0:128], rows[:, 128:256]], axis=0)
        drows_send[...] = mm(place_tab[:, pl.ds(P_FAR, 384)], rows).astype(BF16)
        drows_back.start()

    for copy in near_back:
        copy.wait_recv()

    def gather_coarse(h):
        cols = columns(h)
        for kv in (0, 1):
            coarse = jnp.concatenate(
                [
                    recv_grad[kv, pl.ds(0, 32), cols].astype(F32),
                    recv_grad[kv, pl.ds(32, 16), cols].astype(F32)
                    + recv_grad[kv, pl.ds(48, 16), cols].astype(F32),
                ],
                axis=0,
            )
            total = mm(small_tab[pl.ds(T_GATHER, 32), pl.ds(0, 48)], coarse.astype(BF16)).astype(BF16)
            coarse_grad[0, pl.ds(16 * kv, 16), cols] = total[0:16]
            coarse_grad[1, pl.ds(16 * kv, 16), cols] = total[16:32]

    each_head(gather_coarse)
    coarse_store.start()
    coarse_exit.start()
    drows_back.wait_recv()

    for copy in entry + near_copies + near_back + [one_swap, share, part_swap, one_back, coarse_exit] + exits:
        copy.wait_send()
    for copy in (rows_out, sums_back, adj_out, drows_back):
        copy.wait_send()

    @pl.when(core == 1)
    def _():
        for copy in far_copies + far_back:
            copy.wait_send()

    for copy in stores + [coarse_store]:
        copy.wait()
    for copy in exit_waits + [coarse_wait]:
        copy.wait_recv()


def last_kernel(
    heads, att_ref, dquery_ref, dkey_ref, dvalue_ref, coarse_ref, far_ref, att_out, dquery_out, dkey_out, dvalue_out
):
    att_out[...] = att_ref[...]
    rows = lax.broadcasted_iota(jnp.int32, (64, 32), 0)
    parents = lax.broadcasted_iota(jnp.int32, (64, 32), 1)

    def among(first, count, span):
        at = parents - first
        return (at >= 0) & (at < count) & (rows >= span * at) & (rows < span * at + span)

    spread = jnp.where(among(0, 16, 4), 0.5, 0.0).astype(BF16)[:, 0:16]
    far = [
        jnp.where(among(4 * x, 4, 16), 0.25, 0.0)
        + jnp.where(among(16 + 4 * x, 2, 32), 2.0**-2.5, 0.0)
        + jnp.where(among(18 + 4 * x, 1, 64), 2.0**-3, 0.0)
        + jnp.where(among(19 + 4 * x, 1, 64), 2.0**-3.5, 0.0)
        for x in range(3)
    ]
    far = jnp.concatenate(far, axis=0).astype(BF16)
    for h in range(heads):
        cols = pl.ds(DH * h, DH)
        added = mm(far, far_ref[pl.ds(32 * h, 32)])
        near = [mm(spread, coarse_ref[pl.ds(16 * kv, 16), cols]) for kv in (0, 1)]
        dkey_out[:, cols] = (dkey_ref[:, cols].astype(F32) + added[0:64] + near[0]).astype(BF16)
        dvalue_out[:, cols] = (dvalue_ref[:, cols].astype(F32) + added[64:128] + near[1]).astype(BF16)
        dquery_out[:, cols] = (dquery_ref[:, cols].astype(F32) + added[128:192]).astype(BF16)


def solution(mesh):
    small, halves, places, singles = tables()
    small, halves, places = (table.astype(BF16) for table in (small, halves, places))

    def local(queries, key_rows, values, out_grad):
        rows, columns = queries.shape
        width = columns // 2
        heads = width // DH
        tall = 2 * rows
        anywhere = pl.BlockSpec(memory_space=pl.ANY)
        out = jax.ShapeDtypeStruct((rows, columns), BF16)
        vmem = pltpu.VMEM
        scratch = [
            vmem((192, 256), BF16),
            vmem((768, 512), BF16),
            vmem((512, 768), BF16),
            vmem((S_ROWS, 256), F32),
            vmem((3 * rows, columns), BF16),
            vmem((4, tall, width), BF16),
            vmem((2, 112, width), BF16),
            vmem((112, width), BF16),
            vmem((2, 64, width), BF16),
            vmem((2, 2, 64, width), BF16),
            vmem((2 * heads, 2, 16, 128), BF16),
            vmem((PLANE * 32, 128), BF16),
            vmem((128, 128), BF16),
            vmem((112, 256), BF16),
            vmem((192, 256), BF16),
            vmem((128, 256), BF16),
            vmem((heads, 128, 128), F32),
            vmem((heads, 128, 128), F32),
            vmem((heads, 64, 64), F32),
            vmem((heads, 48, 128), F32),
            vmem((128, 192), F32),
            vmem((heads, 112, 128), F32),
            vmem((heads, 8, 128), F32),
            vmem((heads, 8, 128), F32),
            vmem((PLANE * 16, 128), F32),
            vmem((heads, 2, 16, 128), F32),
            vmem((heads, 2, 16, 128), F32),
            vmem((PLANE * 16, 128), F32),
            vmem((128, 128), BF16),
            vmem((PLANE * 32, 128), BF16),
            vmem((192, 256), BF16),
            vmem((192, 256), BF16),
            vmem((tall, width), BF16),
            vmem((tall, width), BF16),
            vmem((2, tall, width), BF16),
            vmem((heads, 128, 128), BF16),
            vmem((heads, 128, 128), BF16),
            vmem((heads, 128, 128), BF16),
            vmem((heads, 128, 128), F32),
            vmem((heads, 112, 128), F32),
            vmem((2, 2, 64, width), BF16),
            vmem((2, 64, width), BF16),
            vmem((2, 64, width), BF16),
            vmem((2, 64, width), BF16),
            vmem((2, 64, width), BF16),
            vmem((2, 64, width), BF16),
            vmem((2, 32, width), BF16),
            pltpu.SemaphoreType.DMA((11,)),
            pltpu.SemaphoreType.DMA((5,)),
            pltpu.SemaphoreType.DMA((4,)),
            pltpu.SemaphoreType.DMA((COPIES,)),
            pltpu.SemaphoreType.DMA((COPIES,)),
        ]
        parts = pl.pallas_call(
            functools.partial(kernel, heads),
            out_shape=(out,) * 4
            + (jax.ShapeDtypeStruct((32, columns), BF16), jax.ShapeDtypeStruct((64 * heads, 128), BF16)),
            in_specs=[anywhere] * 8,
            out_specs=(anywhere,) * 6,
            scratch_shapes=scratch,
            compiler_params=pltpu.CompilerParams(
                collective_id=0, has_side_effects=True, vmem_limit_bytes=60 << 20
            ),
            name="sibling_attention",
        )(key_rows, values, queries, out_grad, *(jnp.asarray(table) for table in (small, halves, places, singles)))
        whole = pl.BlockSpec(memory_space=pltpu.VMEM)
        return pl.pallas_call(
            functools.partial(last_kernel, 2 * heads),
            out_shape=(out,) * 4,
            in_specs=[whole] * 6,
            out_specs=(whole,) * 4,
            name="coarse_rows_added",
        )(*parts)

    spec = P(("seq", "head"), None)
    return jax.shard_map(
        local, mesh=mesh, in_specs=(spec,) * 4, out_specs=(spec,) * 4, check_vma=False
    )
```
